32 devices in a mesh: group: 2 (over x), island: 16 (over z, y, core).
Axes of the slice: x: 2, y: 2, z: 4, core: 2. Of those that a mesh axis runs over, the one named last changes fastest.
Arguments:
- particles: bfloat16 [256, 4, 8192], P(('group', 'island')), parts along dimension 0, may hold values from -6 to 6
- ancestors: int32 [2, 32, 8], P(None, ('group', 'island')), parts along dimension 1, may hold values from 0 to 15, as said below
- migration: int32 [2, 32, 8], P(None, ('group', 'island')), parts along dimension 1, may hold values from 0 to 7, each once within a row
- pattern: int32 [256, 5], P('group'), parts along dimension 0, may hold values from 0 to 127, as said below
- coupling: bfloat16 [256, 5, 4096], P('group'), parts along dimension 0, may hold values from -0.3125 to 0.3125
- cell_rate: float32 [16384], P('group'), parts along dimension 0, may hold values from 0.3 to 3
- current: float32 [8], P('group'), parts along dimension 0, may hold values from -1 to 1
- observed: float32 [8, 8192], P('group'), parts along dimension 0, may hold values from -6 to 6
- noise_seeds: int32 [32, 4], P(('group', 'island')), parts along dimension 0, may hold values from 0 to 1048575
Outputs:
- final_states: bfloat16 [256, 4, 8192], P(('group', 'island')), parts along dimension 0
- evidence: float32 [32], P(('group', 'island')), parts along dimension 0
- log_weight: float32 [2, 256], P(None, ('group', 'island')), parts along dimension 1
The draws below stay inside these ranges and needn't reach their ends.
There are 2 independent parts, one for each index of `group`. The reference program is written for one: setup_inputs(seed, part) draws one part's arguments, and reference() takes and returns one part's arrays. A program takes and returns all parts, laid end to end along the dimension named above; each array names one. Nothing has to cross between parts.
Inputs may be any that keep to these rules, and one draw needn't show every extreme that they name: `ancestors`: each entry indexes the 16 particles of the device's island; at most 2 entries of one device and epoch point to the other device of the island, and in every epoch some device has exactly 2 such entries. `migration`: each row of one device and epoch holds every slot once. `pattern`: row b holds b, (b + 1) mod 128, (b - 1) mod 128 and two more block numbers.
All inputs are finite; a program needn't handle non-finite values.
Results may differ from the reference program's by a relative error of at most 0.0056.
Values may be sent and summed in bfloat16 or wider, within the bound.
No kernel may reach another device: no remote copies, remote signals or barrier semaphores. Data moves between devices by JAX's collectives and lax.ppermute only.
A program may use at most 128 MiB of HBM per device.

```python
import math
import jax
import jax.numpy as jnp
from jax import lax

CELLS = 8192
STATES = 4
BLOCK = 64
NEIGH = 5
PD = 8
EPOCHS = 2
STEPS_EPOCH = 2
STEPS = 4
BLOCKS = 128
MIG = 1
CROSS = 2
PARTICLES = 128
N_ISLAND = 16


def ancestor_epoch(epoch_key):
    subkeys = jax.random.split(epoch_key, 5)
    capped = jax.random.randint(subkeys[0], (N_ISLAND,), 0, CROSS + 1)
    forced = jax.random.randint(subkeys[1], (), 0, N_ISLAND)
    device_ids = jnp.arange(N_ISLAND)
    capped = jnp.where(device_ids == forced, CROSS, capped)
    device_keys = jax.random.split(subkeys[2], N_ISLAND)
    ranking = jax.vmap(lambda device_key: jax.random.permutation(device_key, PD))(device_keys)
    is_cross = ranking < capped[:, None]
    first_pick = jax.random.randint(subkeys[3], (N_ISLAND, PD), 0, PD)
    second = jax.random.randint(subkeys[4], (N_ISLAND, PD), 0, PD)
    offset = jnp.minimum(first_pick, second)
    core_half = device_ids % 2
    own_start = core_half * PD
    other_start = (1 - core_half) * PD
    start_slot = jnp.where(is_cross, other_start[:, None], own_start[:, None])
    return (start_slot + offset).astype(jnp.int32)


def draw_ancestors(key, part):
    epoch_keys = jax.random.split(jax.random.fold_in(key, 11), EPOCHS)
    return jax.vmap(ancestor_epoch)(epoch_keys)


def draw_pattern(key, part):
    block_rows = jnp.arange(BLOCKS)
    distant = jax.random.randint(jax.random.fold_in(key, 23), (BLOCKS, 2), 0, BLOCKS)
    nearby = jnp.stack([block_rows, (block_rows + 1) % BLOCKS, (block_rows + BLOCKS - 1) % BLOCKS], axis=1)
    return jnp.concatenate([nearby, distant], axis=1).astype(jnp.int32)


def set_ends(result, own_key, least, top_value):
    index_at = [jax.random.randint(jax.random.fold_in(own_key, axis), (), 0, length) for axis, length in enumerate(result.shape)]
    main_axis = result.shape.index(max(result.shape))
    neighbour = index_at[:main_axis] + [(index_at[main_axis] + 1) % result.shape[main_axis]] + index_at[main_axis + 1:]
    return result.at[tuple(index_at)].set(least).at[tuple(neighbour)].set(top_value)


def steps_of(stream_key, extent, shards, low, top_value):
    def one(position, blocks):
        draws = jax.random.uniform(jax.random.fold_in(jax.random.fold_in(stream_key, 6), position), (blocks,), jnp.float32, low / len(shards), top_value / len(shards))
        return jnp.repeat(jnp.exp(draws), extent[position] // blocks).reshape((-1,) + (1,) * (len(extent) - position - 1))

    gain = one(*shards[0])
    for cut in shards[1:]:
        gain = gain * one(*cut)
    return gain


def centred(stream_key, dims, scale, most, pieces=(), kind=jnp.bfloat16):
    result = scale * jax.random.normal(stream_key, dims, jnp.float32)
    if pieces:
        result = result * steps_of(stream_key, dims, pieces, -0.22, 0.18)
    return jnp.clip(result, -most, most).astype(kind)


def setup_inputs(seed: int = 0, part: int = 0) -> dict:
    streams_of = jax.random.split(jax.random.key(seed), 10)
    part_splits = jax.random.split(jax.random.fold_in(streams_of[9], part), 10)
    particles = centred(part_splits[0], (PARTICLES, STATES, CELLS), 1.0, 6.0, ((0, 16),))
    ancestors = draw_ancestors(jax.random.fold_in(jax.random.fold_in(streams_of[9], part), 71), part)
    migration = jax.vmap(lambda own: jax.random.permutation(own, PD))(jax.random.split(part_splits[2], EPOCHS * N_ISLAND)).reshape((EPOCHS, N_ISLAND, PD)).astype(jnp.int32)
    pattern = draw_pattern(jax.random.fold_in(jax.random.fold_in(streams_of[9], part), 71), part)
    coupling = centred(part_splits[4], (BLOCKS, NEIGH, BLOCK * BLOCK), (NEIGH * BLOCK) ** -0.5, 0.3125)
    cell_rate = jnp.clip(jnp.exp(jax.random.uniform(part_splits[5], (CELLS,), jnp.float32, math.log(0.3), math.log(3.0))), 0.3, 3.0)
    current = jnp.clip(jax.random.uniform(part_splits[6], (STEPS,), jnp.float32, -1.0, 1.0), -1.0, 1.0)
    observed = centred(part_splits[7], (STEPS, CELLS), 1.0, 6.0, (), jnp.float32)
    noise_seeds = set_ends(jax.random.randint(part_splits[8], (N_ISLAND, STEPS), 0, 1048576), jax.random.fold_in(part_splits[8], 1), 0, 1048575).astype(jnp.int32)
    return {"particles": particles, "ancestors": ancestors, "migration": migration, "pattern": pattern, "coupling": coupling, "cell_rate": cell_rate, "current": current, "observed": observed, "noise_seeds": noise_seeds}


def scramble(hashed):
    shifter = jnp.full(hashed.shape, 16, jnp.int32)
    hashed = hashed ^ lax.shift_right_logical(hashed, shifter)
    hashed = hashed * 73244475
    hashed = hashed ^ lax.shift_right_logical(hashed, shifter)
    hashed = hashed * 73244475
    hashed = hashed ^ lax.shift_right_logical(hashed, shifter)
    return (hashed & 16777215).astype(jnp.float32) * (1.0 / 16777216.0)

def make_noise(seed_value, row_count):
    counter = jnp.arange(row_count * STATES * CELLS, dtype=jnp.int32).reshape(row_count, STATES, CELLS)
    anchor = counter * 2 + seed_value * 40503
    return (scramble(anchor) - scramble(anchor + 1)) * 2.449489742783178

def couple(stored, coupling, pattern):
    row_count = stored.shape[0] * STATES
    blocked = stored.reshape(row_count, BLOCKS, BLOCK).astype(jnp.float32)
    weights = coupling.reshape(BLOCKS, NEIGH, BLOCK, BLOCK).astype(jnp.float32)
    summed = jnp.zeros((row_count, BLOCKS, BLOCK), jnp.float32)
    for neighbor in range(NEIGH):
        picked = jnp.take(blocked, pattern[:, neighbor], axis=1)
        summed = summed + jnp.einsum('rbi,bio->rbo', picked, weights[:, neighbor], precision=lax.Precision.HIGHEST)
    return summed.reshape(stored.shape)

def advance(stored, coupling, pattern, cell_rate, current_now, observed_now, seed_value, temper_value):
    row_count = stored.shape[0]
    mixed_field = 0.6 * stored.astype(jnp.float32) + 0.8 * couple(stored, coupling, pattern)
    noise_field = make_noise(seed_value, row_count)
    charge_latent = mixed_field[:, 0]
    over_latent = mixed_field[:, 1]
    heat_latent = mixed_field[:, 2]
    film_latent = mixed_field[:, 3]
    charge = jax.nn.sigmoid(charge_latent)
    reaction = cell_rate * jnp.exp(0.6 * jnp.tanh(heat_latent)) * jnp.sqrt(charge * (1.0 - charge)) * jnp.sinh(2.0 * jnp.tanh(over_latent))
    new_charge = charge_latent - 0.25 * reaction + 0.3 * noise_field[:, 0]
    new_over = 0.7 * over_latent + 0.5 * (current_now - reaction) + 0.3 * noise_field[:, 1]
    new_heat = 0.9 * heat_latent + 0.2 * reaction * jnp.tanh(over_latent) + 0.3 * noise_field[:, 2]
    new_film = 0.95 * film_latent + 0.02 * reaction * reaction + 0.3 * noise_field[:, 3]
    predicted = jax.nn.sigmoid(new_charge) - 0.4 * jnp.tanh(new_over) - 0.2 * new_film * current_now
    misfit = observed_now - predicted
    gained = -0.5 * temper_value * lax.optimization_barrier(jnp.sum(misfit * misfit, axis=1))
    stacked = jnp.stack([new_charge, new_over, new_heat, new_film], axis=1).astype(jnp.bfloat16)
    return (stacked, gained)

def take_rows(source_pool, chosen):
    return jnp.take(source_pool, chosen, axis=0)

def put_rows(target_pool, chosen, incoming):
    return target_pool.at[chosen].set(incoming)

def reference(particles, ancestors, migration, pattern, coupling, cell_rate, current, observed, noise_seeds):
    states = particles.reshape(N_ISLAND, PD, STATES, CELLS)
    device_ids = jnp.arange(N_ISLAND, dtype=jnp.int32)
    temper = 0.25 * jnp.power(2.0, (device_ids // 2 % 4).astype(jnp.float32))
    evidence = jnp.zeros((N_ISLAND,), jnp.float32)
    weight_rows = []
    for epoch_index in range(EPOCHS):
        island_view = states.reshape(N_ISLAND // 2, 2 * PD, STATES, CELLS)
        picks = ancestors[epoch_index].reshape(N_ISLAND // 2, 2 * PD).astype(jnp.int32)
        states = jax.vmap(take_rows)(island_view, picks).reshape(N_ISLAND, PD, STATES, CELLS)
        mig_slots = migration[epoch_index, :, :MIG].astype(jnp.int32)
        leaving = jax.vmap(take_rows)(states, mig_slots)
        arriving = jnp.roll(leaving, 2, axis=0)
        states = jax.vmap(put_rows)(states, mig_slots, arriving)
        loglik = jnp.zeros((N_ISLAND, PD), jnp.float32)
        for inner_step in range(STEPS_EPOCH):
            step_index = epoch_index * STEPS_EPOCH + inner_step

            def one_device(packed):
                device_states, seed_value, temper_value = packed
                return advance(device_states, coupling, pattern, cell_rate, current[step_index], observed[step_index], seed_value, temper_value)
            states, gained = lax.map(one_device, (states, noise_seeds[:, step_index], temper))
            loglik = loglik + gained
        island_ll = loglik.reshape(N_ISLAND // 2, 2 * PD)
        island_peak = lax.optimization_barrier(jnp.max(island_ll, axis=1, keepdims=True))
        island_lse = island_peak[:, 0] + jnp.log(lax.optimization_barrier(jnp.sum(jnp.exp(island_ll - island_peak), axis=1)))
        weight_rows.append((island_ll - island_lse[:, None]).reshape(N_ISLAND * PD))
        evidence = evidence + jnp.repeat((island_lse - jnp.log(2.0 * PD)) / CELLS, 2)
    log_weight = jnp.stack(weight_rows, axis=0)
    return (states.reshape(N_ISLAND * PD, STATES, CELLS), evidence, log_weight)
```

```python
import functools

import jax
import jax.numpy as jnp
from jax import lax
from jax.experimental import pallas as pl
from jax.experimental.pallas import tpu as pltpu
from jax.sharding import PartitionSpec as P

CELLS = 8192
STATES = 4
BLOCK = 64
NEIGH = 5
EPOCHS = 2
STEPS_EPOCH = 2
STEPS = EPOCHS * STEPS_EPOCH
BLOCKS = 128
ROWS = 8
LANES = 128
PAIRS = CELLS // LANES
HALF = BLOCK // 2
NOISE_SCALE = 0.3 * 2.449489742783178 / 16777216.0

VMEM = pl.BlockSpec(memory_space=pltpu.VMEM)
SMEM = pl.BlockSpec(memory_space=pltpu.SMEM)
HBM = pl.BlockSpec(memory_space=pl.ANY)


def params(mib):
    return pltpu.CompilerParams(vmem_limit_bytes=mib << 20)


def from_partner(value):
    pairs = [(source, source ^ 1) for source in range(lax.axis_size("island"))]
    return lax.ppermute(value, "island", pairs)


def from_behind(block):
    count = lax.axis_size("island")
    route = [((i - 2) % count, i) for i in range(count)]
    return lax.ppermute(block, "island", route)


def shifted(hashed):
    return hashed ^ lax.shift_right_logical(hashed, jnp.full(hashed.shape, 16, jnp.int32))


def scramble(hashed):
    hashed = shifted(hashed) * 73244475
    hashed = shifted(hashed) * 73244475
    return shifted(hashed) & 16777215


def noise_kernel(seeds, out):
    row = lax.broadcasted_iota(jnp.int32, (STATES * ROWS, LANES), 0)
    lane = lax.broadcasted_iota(jnp.int32, (STATES * ROWS, LANES), 1)
    counter = 2 * (((row % ROWS) * STATES + row // ROWS) * CELLS + lane)
    for step in range(STEPS):
        start = counter + seeds[0, step] * 40503

        def one(q, carry):
            anchor = start + q * (2 * LANES)
            apart = scramble(anchor) - scramble(anchor + 1)
            out[step, q] = apart.astype(jnp.float32) * NOISE_SCALE
            return carry

        lax.fori_loop(0, PAIRS, one, 0, unroll=4)


def weights_kernel(coupling, out, wide):
    group = 16

    def one(g, carry):
        for k in range(NEIGH):
            for r in range(HALF):
                wide[k, r * group : (r + 1) * group, :] = coupling[
                    k, pl.ds(pl.multiple_of(g * group, group), group), r * LANES : (r + 1) * LANES
                ].astype(jnp.float32)
            for b in range(group):
                picked = wide[k, pl.ds(b, HALF, stride=group), :]
                out[g * group + b, k * HALF : (k + 1) * HALF, :] = picked.astype(jnp.bfloat16)
        return carry

    lax.fori_loop(0, BLOCKS // group, one, 0)


def leaving_kernel(epoch, ancestors, migration, half, local, partner, out, sem):
    chosen = ancestors[epoch, 0, migration[epoch, 0, 0]]
    slot = chosen % ROWS
    is_local = chosen // ROWS == half[0]

    @pl.when(is_local)
    def _():
        copy = pltpu.make_async_copy(local.at[pl.ds(slot, 1)], out, sem)
        copy.start()
        copy.wait()

    @pl.when(jnp.logical_not(is_local))
    def _():
        copy = pltpu.make_async_copy(partner.at[pl.ds(slot, 1)], out, sem)
        copy.start()
        copy.wait()


def epoch_kernel(
    epoch,
    ancestors,
    migration,
    half,
    pattern,
    current,
    temper,
    local,
    partner,
    arriving,
    weights,
    noise,
    cell_rate,
    observed,
    *rest,
):
    if epoch:
        before, states, logliks, gather, natural, spread, unmix, total = rest
    else:
        states, logliks, gather, natural, spread, unmix, total = rest
    lane = lax.broadcasted_iota(jnp.int32, (1, LANES), 1)

    source = lax.broadcasted_iota(jnp.int32, (LANES, 4 * LANES), 0)
    target = lax.broadcasted_iota(jnp.int32, (LANES, 4 * LANES), 1)
    tile = target // LANES
    wanted = (tile // 2) * BLOCK + (target % HALF) * 2 + tile % 2
    unmix[...] = jnp.where(source == wanted, 1.0, 0.0).astype(jnp.bfloat16)

    picks = []
    for j in range(ROWS):
        chosen = ancestors[epoch, 0, j]
        picks.append((chosen % ROWS, chosen // ROWS == half[0], migration[epoch, 0, 0] == j))

    def assemble(q, carry):
        lanes = pl.ds(pl.multiple_of(q * LANES, LANES), LANES)
        for j, (slot, is_local, is_new) in enumerate(picks):
            kept = jnp.where(
                is_local, local[slot, :, lanes].astype(jnp.float32), partner[slot, :, lanes].astype(jnp.float32)
            )
            gather[q, j * STATES : (j + 1) * STATES, :] = jnp.where(
                is_new, arriving[0, :, lanes].astype(jnp.float32), kept
            )
        for c in range(0, STATES, 2):
            two = [gather[q, pl.ds(c + d, ROWS, stride=STATES), :] for d in range(2)]
            natural[q, c * ROWS : (c + 2) * ROWS, :] = jnp.concatenate(two, axis=0).astype(jnp.bfloat16)
        return carry

    lax.fori_loop(0, PAIRS, assemble, 0, unroll=4)

    rows = STATES * ROWS

    def spread_out():
        chunk = 8

        def one(g, carry):
            cells = natural[pl.ds(g * chunk, chunk)].reshape(chunk * rows, LANES)
            placed = jnp.dot(cells, unmix[...], preferred_element_type=jnp.float32).astype(jnp.bfloat16)
            for q in range(chunk):
                for tile in range(4):
                    spread[
                        2 * (g * chunk + q) + tile // 2, (tile % 2) * rows : (tile % 2 + 1) * rows, :
                    ] = placed[q * rows : (q + 1) * rows, tile * LANES : (tile + 1) * LANES]
            return carry

        lax.fori_loop(0, PAIRS // chunk, one, 0)

    def product(b):
        pieces = [spread[pattern[k, b]] for k in range(NEIGH)]
        first = jnp.where(
            lane < HALF,
            pieces[0],
            jnp.where(lane < 2 * HALF, pieces[1], jnp.where(lane < 3 * HALF, pieces[2], pieces[3])),
        )
        both = jnp.concatenate([first, pieces[4][:, :HALF]], axis=1)
        return jnp.dot(both, weights[b], preferred_element_type=jnp.float32)

    for inner in range(STEPS_EPOCH):
        step = epoch * STEPS_EPOCH + inner
        last = inner == STEPS_EPOCH - 1
        now = current[step]
        spread_out()
        total[...] = jnp.zeros_like(total) if inner == 0 else total[...]

        def one(q, carry):
            left = product(2 * q)
            right = product(2 * q + 1)
            inside = jnp.where(lane < BLOCK, left[:rows], right[rows:])
            across = jnp.where(lane < BLOCK, right[:rows], left[rows:])
            coupled = inside + pltpu.roll(across, BLOCK, 1)
            mixed = 0.6 * natural[q].astype(jnp.float32) + 0.8 * coupled
            drawn = noise[step, q]
            charge, over, heat, film = (mixed[c * ROWS : (c + 1) * ROWS] for c in range(STATES))
            rate = cell_rate[pl.ds(q, 1), :]
            seen = observed[step, pl.ds(q, 1), :]
            tanh_over = jnp.tanh(over)
            fade = jnp.exp(-0.5 * jnp.abs(charge))
            warm = 0.6 * jnp.tanh(heat)
            rise = jnp.exp(warm + 2.0 * tanh_over) - jnp.exp(warm - 2.0 * tanh_over)
            reaction = (0.5 * rate) * rise * fade / (1.0 + fade * fade)
            new_charge = charge - 0.25 * reaction + drawn[:ROWS]
            new_over = 0.7 * over + 0.5 * (now - reaction) + drawn[ROWS : 2 * ROWS]
            new_heat = 0.9 * heat + 0.2 * reaction * tanh_over + drawn[2 * ROWS : 3 * ROWS]
            new_film = 0.95 * film + 0.02 * reaction * reaction + drawn[3 * ROWS :]
            predicted = (
                0.5 + 0.5 * jnp.tanh(0.5 * new_charge) - 0.4 * jnp.tanh(new_over) - (0.2 * now) * new_film
            )
            misfit = seen - predicted
            fresh = (new_charge, new_over, new_heat, new_film)
            if last:
                for c in range(STATES):
                    gather[q, pl.ds(c, ROWS, stride=STATES), :] = fresh[c]
            else:
                natural[q] = jnp.concatenate(fresh, axis=0).astype(jnp.bfloat16)
            return carry + misfit * misfit

        total[...] += lax.fori_loop(0, PAIRS, one, jnp.zeros((ROWS, LANES), jnp.float32), unroll=4)

    def finish(q, carry):
        lanes = pl.ds(pl.multiple_of(q * LANES, LANES), LANES)
        for j in range(ROWS):
            states[j, :, lanes] = gather[q, j * STATES : (j + 1) * STATES, :].astype(jnp.bfloat16)
        return carry

    lax.fori_loop(0, PAIRS, finish, 0, unroll=4)

    column = -0.5 * temper[0] * jnp.sum(total[...], axis=1, keepdims=True)
    slots = lax.broadcasted_iota(jnp.int32, (ROWS, LANES), 0)
    across_lanes = jnp.sum(jnp.where(slots == lane, column, 0.0), axis=0, keepdims=True)
    if epoch:
        logliks[0:1, :] = before[0:1, :]
    logliks[epoch : epoch + 1, :] = across_lanes


def weigh_kernel(own, other, log_weight, evidence):
    lane = lax.broadcasted_iota(jnp.int32, (EPOCHS, LANES), 1)
    real = lane < ROWS
    mine, theirs = own[...], other[...]
    peak = jnp.max(jnp.where(real, jnp.maximum(mine, theirs), -jnp.inf), axis=1, keepdims=True)
    shares = jnp.where(real, jnp.exp(mine - peak) + jnp.exp(theirs - peak), 0.0)
    lse = peak + jnp.log(jnp.sum(shares, axis=1, keepdims=True))
    log_weight[...] = (mine - lse)[:, :ROWS]
    per_cell = (lse - jnp.log(jnp.full(lse.shape, 2.0 * ROWS, jnp.float32))) / CELLS
    evidence[...] = jnp.sum(per_cell, axis=0, keepdims=True)


def on_device(
    particles, ancestors, migration, pattern, coupling, cell_rate, current, observed, noise_seeds
):
    position = lax.axis_index("island")
    half = (position % 2).astype(jnp.int32)[None]
    temper = (0.25 * jnp.power(2.0, (position // 2 % 4).astype(jnp.float32)))[None]
    shape = jax.ShapeDtypeStruct

    noise = pl.pallas_call(
        noise_kernel,
        out_shape=shape((STEPS, PAIRS, STATES * ROWS, LANES), jnp.float32),
        in_specs=[SMEM],
        out_specs=VMEM,
        compiler_params=params(2),
        cost_estimate=pl.CostEstimate(flops=30000000, bytes_accessed=12000000, transcendentals=0),
        name="noise",
    )(noise_seeds)
    weights = pl.pallas_call(
        weights_kernel,
        out_shape=shape((BLOCKS, NEIGH * HALF, LANES), jnp.bfloat16),
        in_specs=[VMEM],
        out_specs=VMEM,
        scratch_shapes=[pltpu.VMEM((NEIGH, HALF * 16, LANES), jnp.float32)],
        compiler_params=params(4),
        cost_estimate=pl.CostEstimate(flops=3000000, bytes_accessed=10000000, transcendentals=0),
        name="weights",
    )(coupling.transpose(1, 0, 2))

    states = particles
    logliks = ()
    rates = cell_rate.reshape(PAIRS, LANES)
    seen = observed.reshape(STEPS, PAIRS, LANES)
    for epoch in range(EPOCHS):
        partner = from_partner(states)
        leaving = pl.pallas_call(
            functools.partial(leaving_kernel, epoch),
            out_shape=shape((1, STATES, CELLS), jnp.bfloat16),
            in_specs=[SMEM, SMEM, SMEM, HBM, HBM],
            out_specs=HBM,
            scratch_shapes=[pltpu.SemaphoreType.DMA],
            compiler_params=params(1),
            name="leaving",
        )(ancestors, migration, half, states, partner)
        arriving = from_behind(leaving)
        states, logliks = pl.pallas_call(
            functools.partial(epoch_kernel, epoch),
            out_shape=(
                shape((ROWS, STATES, CELLS), jnp.bfloat16),
                shape((EPOCHS, LANES), jnp.float32),
            ),
            in_specs=[SMEM] * 6 + [VMEM] * (8 if epoch else 7),
            out_specs=(VMEM, VMEM),
            scratch_shapes=[
                pltpu.VMEM((PAIRS, STATES * ROWS, LANES), jnp.float32),
                pltpu.VMEM((PAIRS, STATES * ROWS, LANES), jnp.bfloat16),
                pltpu.VMEM((BLOCKS, 2 * STATES * ROWS, LANES), jnp.bfloat16),
                pltpu.VMEM((LANES, 4 * LANES), jnp.bfloat16),
                pltpu.VMEM((ROWS, LANES), jnp.float32),
            ],
            compiler_params=params(12),
            name="epoch",
        )(
            ancestors,
            migration,
            half,
            pattern.T,
            current,
            temper,
            states,
            partner,
            arriving,
            weights,
            noise,
            rates,
            seen,
            *([logliks] if epoch else []),
        )
    log_weight, evidence = pl.pallas_call(
        weigh_kernel,
        out_shape=(shape((EPOCHS, ROWS), jnp.float32), shape((1, 1), jnp.float32)),
        in_specs=[VMEM, VMEM],
        out_specs=(VMEM, VMEM),
        compiler_params=params(1),
        name="weigh",
    )(logliks, from_partner(logliks))
    return (states, evidence.reshape(1), log_weight)


def solution(mesh):
    return jax.shard_map(
        on_device,
        mesh=mesh,
        in_specs=(
            P(("group", "island"), None, None),
            P(None, ("group", "island"), None),
            P(None, ("group", "island"), None),
            P("group", None),
            P("group", None, None),
            P("group"),
            P("group"),
            P("group", None),
            P(("group", "island"), None),
        ),
        out_specs=(
            P(("group", "island"), None, None),
            P(("group", "island")),
            P(None, ("group", "island")),
        ),
        check_vma=False,
    )
```

```python
import functools

import jax
import jax.numpy as jnp
from jax import lax
from jax.experimental import pallas as pl
from jax.experimental.pallas import tpu as pltpu
from jax.sharding import PartitionSpec as P

CELLS = 8192
STATES = 4
BLOCK = 64
NEIGH = 5
EPOCHS = 2
STEPS_EPOCH = 2
STEPS = EPOCHS * STEPS_EPOCH
BLOCKS = 128
ROWS = 8
LANES = 128
GROUP = 16
PAIRS = CELLS // LANES
HALF = BLOCK // 2
NOISE_SCALE = 0.3 * 2.449489742783178 / 16777216.0

VMEM = pl.BlockSpec(memory_space=pltpu.VMEM)
SMEM = pl.BlockSpec(memory_space=pltpu.SMEM)
HBM = pl.BlockSpec(memory_space=pl.ANY)


def params(mib):
    return pltpu.CompilerParams(vmem_limit_bytes=mib << 20)


def from_partner(value):
    pairs = [(source, source ^ 1) for source in range(lax.axis_size("island"))]
    return lax.ppermute(value, "island", pairs)


def from_behind(block):
    count = lax.axis_size("island")
    route = [((i - 2) % count, i) for i in range(count)]
    return lax.ppermute(block, "island", route)


def shifted(hashed):
    return hashed ^ lax.shift_right_logical(hashed, jnp.full(hashed.shape, 16, jnp.int32))


def scramble(hashed):
    hashed = shifted(hashed) * 73244475
    hashed = shifted(hashed) * 73244475
    return shifted(hashed) & 16777215


def noise_kernel(seeds, out):
    row = lax.broadcasted_iota(jnp.int32, (STATES * ROWS, LANES), 0)
    lane = lax.broadcasted_iota(jnp.int32, (STATES * ROWS, LANES), 1)
    counter = 2 * (((row % ROWS) * STATES + row // ROWS) * CELLS + lane)
    for step in range(STEPS):
        start = counter + seeds[0, step] * 40503

        def one(q, carry):
            anchor = start + q * (2 * LANES)
            apart = scramble(anchor) - scramble(anchor + 1)
            out[step, q] = apart.astype(jnp.float32) * NOISE_SCALE
            return carry

        lax.fori_loop(0, PAIRS, one, 0, unroll=4)


def weights_kernel(coupling, out, wide):
    group = 16

    def one(g, carry):
        for k in range(NEIGH):
            for r in range(HALF):
                wide[k, r * group : (r + 1) * group, :] = coupling[
                    k, pl.ds(pl.multiple_of(g * group, group), group), r * LANES : (r + 1) * LANES
                ].astype(jnp.float32)
            for b in range(group):
                picked = wide[k, pl.ds(b, HALF, stride=group), :]
                out[g * group + b, k * HALF : (k + 1) * HALF, :] = picked.astype(jnp.bfloat16)
        return carry

    lax.fori_loop(0, BLOCKS // group, one, 0)


def leaving_kernel(epoch, ancestors, migration, half, local, partner, out, sem):
    chosen = ancestors[epoch, 0, migration[epoch, 0, 0]]
    slot = chosen % ROWS
    is_local = chosen // ROWS == half[0]

    @pl.when(is_local)
    def _():
        copy = pltpu.make_async_copy(local.at[pl.ds(slot, 1)], out, sem)
        copy.start()
        copy.wait()

    @pl.when(jnp.logical_not(is_local))
    def _():
        copy = pltpu.make_async_copy(partner.at[pl.ds(slot, 1)], out, sem)
        copy.start()
        copy.wait()


def members(g):
    return [g * GROUP + i for i in range(GROUP)]


def in_turn(*stages):
    count = PAIRS // GROUP
    depth = len(stages)

    def one(at, low, high):
        for s in reversed(range(low, high)):
            stages[s](at - s)

    def steady(at, carry):
        one(at, 0, depth)
        return carry

    for at in range(depth - 1):
        one(at, 0, at + 1)
    lax.fori_loop(depth - 1, count, steady, 0)
    for at in range(count, count + depth - 1):
        one(at, at - count + 1, depth)


def epoch_kernel(
    epoch,
    ancestors,
    migration,
    half,
    pattern,
    current,
    temper,
    local,
    partner,
    arriving,
    weights,
    noise,
    cell_rate,
    observed,
    *rest,
):
    if epoch:
        before, *rest = rest
    states, logliks, gather, natural, spread, spread_next, coupled, unmix, total = rest
    lane = lax.broadcasted_iota(jnp.int32, (1, LANES), 1)

    source = lax.broadcasted_iota(jnp.int32, (LANES, 4 * LANES), 0)
    target = lax.broadcasted_iota(jnp.int32, (LANES, 4 * LANES), 1)
    tile = target // LANES
    wanted = (tile // 2) * BLOCK + (target % HALF) * 2 + tile % 2
    unmix[...] = jnp.where(source == wanted, 1.0, 0.0).astype(jnp.bfloat16)

    picks = []
    for j in range(ROWS):
        chosen = ancestors[epoch, 0, j]
        picks.append((chosen % ROWS, chosen // ROWS == half[0], migration[epoch, 0, 0] == j))

    rows = STATES * ROWS
    total[...] = jnp.zeros_like(total)

    def assemble(g):
        for q in members(g):
            lanes = pl.ds(pl.multiple_of(q * LANES, LANES), LANES)
            for j, (slot, is_local, is_new) in enumerate(picks):
                kept = jnp.where(
                    is_local,
                    local[slot, :, lanes].astype(jnp.float32),
                    partner[slot, :, lanes].astype(jnp.float32),
                )
                gather[q, j * STATES : (j + 1) * STATES, :] = jnp.where(
                    is_new, arriving[0, :, lanes].astype(jnp.float32), kept
                )
            for c in range(0, STATES, 2):
                two = [gather[q, pl.ds(c + d, ROWS, stride=STATES), :] for d in range(2)]
                natural[q, c * ROWS : (c + 2) * ROWS, :] = jnp.concatenate(two, axis=0).astype(
                    jnp.bfloat16
                )

    def spread_out(result, g):
        cells = natural[pl.ds(g * GROUP, GROUP)].reshape(GROUP * rows, LANES)
        placed = jnp.dot(cells, unmix[...], preferred_element_type=jnp.float32).astype(jnp.bfloat16)
        for i, q in enumerate(members(g)):
            for tile in range(4):
                result[2 * q + tile // 2, (tile % 2) * rows : (tile % 2 + 1) * rows, :] = placed[
                    i * rows : (i + 1) * rows, tile * LANES : (tile + 1) * LANES
                ]

    def product(held, b):
        pieces = [held[pattern[k, b]] for k in range(NEIGH)]
        first = jnp.where(
            lane < HALF,
            pieces[0],
            jnp.where(lane < 2 * HALF, pieces[1], jnp.where(lane < 3 * HALF, pieces[2], pieces[3])),
        )
        both = jnp.concatenate([first, pieces[4][:, :HALF]], axis=1)
        return jnp.dot(both, weights[b], preferred_element_type=jnp.float32)

    def couple(held, g):
        for i, q in enumerate(members(g)):
            left = product(held, 2 * q)
            right = product(held, 2 * q + 1)
            inside = jnp.where(lane < BLOCK, left[:rows], right[rows:])
            across = jnp.where(lane < BLOCK, right[:rows], left[rows:])
            coupled[i] = inside + pltpu.roll(across, BLOCK, 1)

    def propagate(step, g):
        now = current[step]
        gained = jnp.zeros((ROWS, LANES), jnp.float32)
        for i, q in enumerate(members(g)):
            mixed = 0.6 * natural[q].astype(jnp.float32) + 0.8 * coupled[i]
            drawn = noise[step, q]
            charge, over, heat, film = (mixed[c * ROWS : (c + 1) * ROWS] for c in range(STATES))
            rate = cell_rate[pl.ds(q, 1), :]
            seen = observed[step, pl.ds(q, 1), :]
            tanh_over = jnp.tanh(over)
            fade = jnp.exp(-0.5 * jnp.abs(charge))
            warm = 0.6 * jnp.tanh(heat)
            rise = jnp.exp(warm + 2.0 * tanh_over) - jnp.exp(warm - 2.0 * tanh_over)
            reaction = (0.5 * rate) * rise * fade / (1.0 + fade * fade)
            new_charge = charge - 0.25 * reaction + drawn[:ROWS]
            new_over = 0.7 * over + 0.5 * (now - reaction) + drawn[ROWS : 2 * ROWS]
            new_heat = 0.9 * heat + 0.2 * reaction * tanh_over + drawn[2 * ROWS : 3 * ROWS]
            new_film = 0.95 * film + 0.02 * reaction * reaction + drawn[3 * ROWS :]
            predicted = (
                0.5 + 0.5 * jnp.tanh(0.5 * new_charge) - 0.4 * jnp.tanh(new_over) - (0.2 * now) * new_film
            )
            misfit = seen - predicted
            gained += misfit * misfit
            fresh = (new_charge, new_over, new_heat, new_film)
            if step % STEPS_EPOCH == STEPS_EPOCH - 1:
                for c in range(STATES):
                    gather[q, pl.ds(c, ROWS, stride=STATES), :] = fresh[c]
            else:
                natural[q] = jnp.concatenate(fresh, axis=0).astype(jnp.bfloat16)
        total[...] += gained

    def finish(g):
        for q in members(g):
            lanes = pl.ds(pl.multiple_of(q * LANES, LANES), LANES)
            for j in range(ROWS):
                states[j, :, lanes] = gather[q, j * STATES : (j + 1) * STATES, :].astype(jnp.bfloat16)

    step = epoch * STEPS_EPOCH
    in_turn(assemble, functools.partial(spread_out, spread))
    in_turn(
        functools.partial(couple, spread),
        functools.partial(propagate, step),
        functools.partial(spread_out, spread_next),
    )
    in_turn(functools.partial(couple, spread_next), functools.partial(propagate, step + 1), finish)

    column = -0.5 * temper[0] * jnp.sum(total[...], axis=1, keepdims=True)
    slots = lax.broadcasted_iota(jnp.int32, (ROWS, LANES), 0)
    across_lanes = jnp.sum(jnp.where(slots == lane, column, 0.0), axis=0, keepdims=True)
    if epoch:
        logliks[0:1, :] = before[0:1, :]
    logliks[epoch : epoch + 1, :] = across_lanes


def weigh_kernel(own, other, log_weight, evidence):
    lane = lax.broadcasted_iota(jnp.int32, (EPOCHS, LANES), 1)
    real = lane < ROWS
    mine, theirs = own[...], other[...]
    peak = jnp.max(jnp.where(real, jnp.maximum(mine, theirs), -jnp.inf), axis=1, keepdims=True)
    shares = jnp.where(real, jnp.exp(mine - peak) + jnp.exp(theirs - peak), 0.0)
    lse = peak + jnp.log(jnp.sum(shares, axis=1, keepdims=True))
    log_weight[...] = (mine - lse)[:, :ROWS]
    per_cell = (lse - jnp.log(jnp.full(lse.shape, 2.0 * ROWS, jnp.float32))) / CELLS
    evidence[...] = jnp.sum(per_cell, axis=0, keepdims=True)


def on_device(
    particles, ancestors, migration, pattern, coupling, cell_rate, current, observed, noise_seeds
):
    position = lax.axis_index("island")
    half = (position % 2).astype(jnp.int32)[None]
    temper = (0.25 * jnp.power(2.0, (position // 2 % 4).astype(jnp.float32)))[None]
    shape = jax.ShapeDtypeStruct

    noise = pl.pallas_call(
        noise_kernel,
        out_shape=shape((STEPS, PAIRS, STATES * ROWS, LANES), jnp.float32),
        in_specs=[SMEM],
        out_specs=VMEM,
        compiler_params=params(2),
        cost_estimate=pl.CostEstimate(flops=30000000, bytes_accessed=12000000, transcendentals=0),
        name="noise",
    )(noise_seeds)
    weights = pl.pallas_call(
        weights_kernel,
        out_shape=shape((BLOCKS, NEIGH * HALF, LANES), jnp.bfloat16),
        in_specs=[VMEM],
        out_specs=VMEM,
        scratch_shapes=[pltpu.VMEM((NEIGH, HALF * 16, LANES), jnp.float32)],
        compiler_params=params(4),
        cost_estimate=pl.CostEstimate(flops=3000000, bytes_accessed=10000000, transcendentals=0),
        name="weights",
    )(coupling.transpose(1, 0, 2))

    states = particles
    logliks = ()
    rates = cell_rate.reshape(PAIRS, LANES)
    seen = observed.reshape(STEPS, PAIRS, LANES)
    for epoch in range(EPOCHS):
        partner = from_partner(states)
        leaving = pl.pallas_call(
            functools.partial(leaving_kernel, epoch),
            out_shape=shape((1, STATES, CELLS), jnp.bfloat16),
            in_specs=[SMEM, SMEM, SMEM, HBM, HBM],
            out_specs=HBM,
            scratch_shapes=[pltpu.SemaphoreType.DMA],
            compiler_params=params(1),
            name="leaving",
        )(ancestors, migration, half, states, partner)
        arriving = from_behind(leaving)
        states, logliks = pl.pallas_call(
            functools.partial(epoch_kernel, epoch),
            out_shape=(
                shape((ROWS, STATES, CELLS), jnp.bfloat16),
                shape((EPOCHS, LANES), jnp.float32),
            ),
            in_specs=[SMEM] * 6 + [VMEM] * (8 if epoch else 7),
            out_specs=(VMEM, VMEM),
            scratch_shapes=[
                pltpu.VMEM((PAIRS, STATES * ROWS, LANES), jnp.float32),
                pltpu.VMEM((PAIRS, STATES * ROWS, LANES), jnp.bfloat16),
                pltpu.VMEM((BLOCKS, 2 * STATES * ROWS, LANES), jnp.bfloat16),
                pltpu.VMEM((BLOCKS, 2 * STATES * ROWS, LANES), jnp.bfloat16),
                pltpu.VMEM((GROUP, STATES * ROWS, LANES), jnp.float32),
                pltpu.VMEM((LANES, 4 * LANES), jnp.bfloat16),
                pltpu.VMEM((ROWS, LANES), jnp.float32),
            ],
            compiler_params=params(12),
            name="epoch",
        )(
            ancestors,
            migration,
            half,
            pattern.T,
            current,
            temper,
            states,
            partner,
            arriving,
            weights,
            noise,
            rates,
            seen,
            *([logliks] if epoch else []),
        )
    log_weight, evidence = pl.pallas_call(
        weigh_kernel,
        out_shape=(shape((EPOCHS, ROWS), jnp.float32), shape((1, 1), jnp.float32)),
        in_specs=[VMEM, VMEM],
        out_specs=(VMEM, VMEM),
        compiler_params=params(1),
        name="weigh",
    )(logliks, from_partner(logliks))
    return (states, evidence.reshape(1), log_weight)


def solution(mesh):
    return jax.shard_map(
        on_device,
        mesh=mesh,
        in_specs=(
            P(("group", "island"), None, None),
            P(None, ("group", "island"), None),
            P(None, ("group", "island"), None),
            P("group", None),
            P("group", None, None),
            P("group"),
            P("group"),
            P("group", None),
            P(("group", "island"), None),
        ),
        out_specs=(
            P(("group", "island"), None, None),
            P(("group", "island")),
            P(None, ("group", "island")),
        ),
        check_vma=False,
    )
```

```python
import functools

import jax
import jax.numpy as jnp
from jax import lax
from jax.experimental import pallas as pl
from jax.experimental.pallas import tpu as pltpu
from jax.sharding import PartitionSpec as P

CELLS = 8192
STATES = 4
BLOCK = 64
NEIGH = 5
EPOCHS = 2
STEPS_EPOCH = 2
STEPS = EPOCHS * STEPS_EPOCH
BLOCKS = 128
ROWS = 8
LANES = 128
GROUP = 16
PAIRS = CELLS // LANES
HALF = BLOCK // 2
NOISE_SCALE = 0.3 * 2.449489742783178 / 16777216.0

VMEM = pl.BlockSpec(memory_space=pltpu.VMEM)
SMEM = pl.BlockSpec(memory_space=pltpu.SMEM)
HBM = pl.BlockSpec(memory_space=pl.ANY)


def in_hbm(array):
    return pltpu.with_memory_space_constraint(array, pltpu.HBM)


def params(mib):
    return pltpu.CompilerParams(vmem_limit_bytes=mib << 20)


def from_partner(value):
    pairs = [(source, source ^ 1) for source in range(lax.axis_size("island"))]
    return lax.ppermute(value, "island", pairs)


def from_behind(block):
    count = lax.axis_size("island")
    route = [((i - 2) % count, i) for i in range(count)]
    return lax.ppermute(block, "island", route)


def shifted(hashed):
    return hashed ^ lax.shift_right_logical(hashed, jnp.full(hashed.shape, 16, jnp.int32))


def scramble(hashed):
    hashed = shifted(hashed) * 73244475
    hashed = shifted(hashed) * 73244475
    return shifted(hashed) & 16777215


def noise_kernel(epoch, seeds, out):
    row = lax.broadcasted_iota(jnp.int32, (STATES * ROWS, LANES), 0)
    lane = lax.broadcasted_iota(jnp.int32, (STATES * ROWS, LANES), 1)
    counter = 2 * (((row % ROWS) * STATES + row // ROWS) * CELLS + lane)
    for step in range(STEPS_EPOCH):
        start = counter + seeds[0, epoch * STEPS_EPOCH + step] * 40503

        def one(q, carry):
            anchor = start + q * (2 * LANES)
            apart = scramble(anchor) - scramble(anchor + 1)
            out[step, q] = apart.astype(jnp.float32) * NOISE_SCALE
            return carry

        lax.fori_loop(0, PAIRS, one, 0, unroll=4)


def weights_kernel(coupling, out, held, wide, sems):
    group = 16

    def fetch(g):
        rows = pl.ds(pl.multiple_of(g * group, group), group)
        return pltpu.make_async_copy(coupling.at[:, rows], held.at[:, rows], sems.at[g])

    for g in range(BLOCKS // group):
        fetch(g).start()

    def one(g, carry):
        fetch(g).wait()
        for k in range(NEIGH):
            for r in range(HALF):
                wide[k, r * group : (r + 1) * group, :] = held[
                    k, pl.ds(pl.multiple_of(g * group, group), group), r * LANES : (r + 1) * LANES
                ].astype(jnp.float32)
            for b in range(group):
                picked = wide[k, pl.ds(b, HALF, stride=group), :]
                out[g * group + b, k * HALF : (k + 1) * HALF, :] = picked.astype(jnp.bfloat16)
        return carry

    lax.fori_loop(0, BLOCKS // group, one, 0)


def leaving_kernel(epoch, ancestors, migration, half, local, partner, out, sem):
    chosen = ancestors[epoch, 0, migration[epoch, 0, 0]]
    slot = chosen % ROWS
    is_local = chosen // ROWS == half[0]

    @pl.when(is_local)
    def _():
        copy = pltpu.make_async_copy(local.at[pl.ds(slot, 1)], out, sem)
        copy.start()
        copy.wait()

    @pl.when(jnp.logical_not(is_local))
    def _():
        copy = pltpu.make_async_copy(partner.at[pl.ds(slot, 1)], out, sem)
        copy.start()
        copy.wait()


def members(g):
    return [g * GROUP + i for i in range(GROUP)]


def in_turn(*stages):
    count = PAIRS // GROUP
    depth = len(stages)

    def one(at, low, high):
        for s in reversed(range(low, high)):
            stages[s](at - s)

    def steady(at, carry):
        one(at, 0, depth)
        return carry

    for at in range(depth - 1):
        one(at, 0, at + 1)
    lax.fori_loop(depth - 1, count, steady, 0)
    for at in range(count, count + depth - 1):
        one(at, at - count + 1, depth)


def epoch_kernel(
    epoch,
    ancestors,
    migration,
    half,
    pattern,
    current,
    temper,
    local,
    partner,
    arriving,
    weights,
    noise,
    cell_rate,
    observed,
    *rest,
):
    if epoch:
        before, *rest = rest
    states, logliks, gather, natural, spread, spread_next, coupled, unmix, total = rest
    lane = lax.broadcasted_iota(jnp.int32, (1, LANES), 1)

    source = lax.broadcasted_iota(jnp.int32, (LANES, 4 * LANES), 0)
    target = lax.broadcasted_iota(jnp.int32, (LANES, 4 * LANES), 1)
    wanted = (target >> 8) * BLOCK + (target & (HALF - 1)) * 2 + ((target >> 7) & 1)
    unmix[...] = jnp.where(source == wanted, 1.0, 0.0).astype(jnp.bfloat16)

    picks = []
    for j in range(ROWS):
        chosen = ancestors[epoch, 0, j]
        picks.append((chosen % ROWS, chosen // ROWS == half[0], migration[epoch, 0, 0] == j))

    rows = STATES * ROWS
    total[...] = jnp.zeros_like(total)

    def assemble(g):
        for q in members(g):
            lanes = pl.ds(pl.multiple_of(q * LANES, LANES), LANES)
            for j, (slot, is_local, is_new) in enumerate(picks):
                kept = jnp.where(
                    is_local,
                    local[slot, :, lanes].astype(jnp.float32),
                    partner[slot, :, lanes].astype(jnp.float32),
                )
                gather[q, j * STATES : (j + 1) * STATES, :] = jnp.where(
                    is_new, arriving[0, :, lanes].astype(jnp.float32), kept
                )
            for c in range(0, STATES, 2):
                two = [gather[q, pl.ds(c + d, ROWS, stride=STATES), :] for d in range(2)]
                natural[q, c * ROWS : (c + 2) * ROWS, :] = jnp.concatenate(two, axis=0).astype(
                    jnp.bfloat16
                )

    def spread_out(result, g):
        cells = natural[pl.ds(g * GROUP, GROUP)].reshape(GROUP * rows, LANES)
        placed = jnp.dot(cells, unmix[...], preferred_element_type=jnp.float32).astype(jnp.bfloat16)
        for i, q in enumerate(members(g)):
            for tile in range(4):
                result[2 * q + tile // 2, (tile % 2) * rows : (tile % 2 + 1) * rows, :] = placed[
                    i * rows : (i + 1) * rows, tile * LANES : (tile + 1) * LANES
                ]

    def product(held, b):
        pieces = [held[pattern[k, b]] for k in range(NEIGH)]
        first = jnp.where(
            lane < HALF,
            pieces[0],
            jnp.where(lane < 2 * HALF, pieces[1], jnp.where(lane < 3 * HALF, pieces[2], pieces[3])),
        )
        both = jnp.concatenate([first, pieces[4][:, :HALF]], axis=1)
        return jnp.dot(both, weights[b], preferred_element_type=jnp.float32)

    def couple(held, g):
        for i, q in enumerate(members(g)):
            left = product(held, 2 * q)
            right = product(held, 2 * q + 1)
            inside = jnp.where(lane < BLOCK, left[:rows], right[rows:])
            across = jnp.where(lane < BLOCK, right[:rows], left[rows:])
            coupled[i] = inside + pltpu.roll(across, BLOCK, 1)

    def propagate(step, g):
        now = current[step]
        gained = jnp.zeros((ROWS, LANES), jnp.float32)
        for i, q in enumerate(members(g)):
            mixed = 0.6 * natural[q].astype(jnp.float32) + 0.8 * coupled[i]
            drawn = noise[step % STEPS_EPOCH, q]
            charge, over, heat, film = (mixed[c * ROWS : (c + 1) * ROWS] for c in range(STATES))
            rate = cell_rate[pl.ds(q, 1), :]
            seen = observed[step : step + 1, pl.ds(pl.multiple_of(q * LANES, LANES), LANES)]
            tanh_over = jnp.tanh(over)
            fade = jnp.exp(-0.5 * jnp.abs(charge))
            warm = 0.6 * jnp.tanh(heat)
            rise = jnp.exp(warm + 2.0 * tanh_over) - jnp.exp(warm - 2.0 * tanh_over)
            reaction = (0.5 * rate) * rise * fade / (1.0 + fade * fade)
            new_charge = charge - 0.25 * reaction + drawn[:ROWS]
            new_over = 0.7 * over + 0.5 * (now - reaction) + drawn[ROWS : 2 * ROWS]
            new_heat = 0.9 * heat + 0.2 * reaction * tanh_over + drawn[2 * ROWS : 3 * ROWS]
            new_film = 0.95 * film + 0.02 * reaction * reaction + drawn[3 * ROWS :]
            predicted = (
                0.5 + 0.5 * jnp.tanh(0.5 * new_charge) - 0.4 * jnp.tanh(new_over) - (0.2 * now) * new_film
            )
            misfit = seen - predicted
            gained += misfit * misfit
            fresh = (new_charge, new_over, new_heat, new_film)
            if step % STEPS_EPOCH == STEPS_EPOCH - 1:
                for c in range(STATES):
                    gather[q, pl.ds(c, ROWS, stride=STATES), :] = fresh[c]
            else:
                natural[q] = jnp.concatenate(fresh, axis=0).astype(jnp.bfloat16)
        total[...] += gained

    def finish(g):
        for q in members(g):
            lanes = pl.ds(pl.multiple_of(q * LANES, LANES), LANES)
            for j in range(ROWS):
                states[j, :, lanes] = gather[q, j * STATES : (j + 1) * STATES, :].astype(jnp.bfloat16)

    step = epoch * STEPS_EPOCH
    in_turn(assemble, functools.partial(spread_out, spread))
    in_turn(
        functools.partial(couple, spread),
        functools.partial(propagate, step),
        functools.partial(spread_out, spread_next),
    )
    in_turn(functools.partial(couple, spread_next), functools.partial(propagate, step + 1), finish)

    column = -0.5 * temper[0] * jnp.sum(total[...], axis=1, keepdims=True)
    slots = lax.broadcasted_iota(jnp.int32, (ROWS, LANES), 0)
    across_lanes = jnp.sum(jnp.where(slots == lane, column, 0.0), axis=0, keepdims=True)
    if epoch:
        logliks[0:1, :] = before[0:1, :]
    logliks[epoch : epoch + 1, :] = across_lanes


def weigh_kernel(own, other, log_weight, evidence):
    lane = lax.broadcasted_iota(jnp.int32, (EPOCHS, LANES), 1)
    real = lane < ROWS
    mine, theirs = own[...], other[...]
    peak = jnp.max(jnp.where(real, jnp.maximum(mine, theirs), -jnp.inf), axis=1, keepdims=True)
    shares = jnp.where(real, jnp.exp(mine - peak) + jnp.exp(theirs - peak), 0.0)
    lse = peak + jnp.log(jnp.sum(shares, axis=1, keepdims=True))
    log_weight[...] = (mine - lse)[:, :ROWS]
    per_cell = (lse - jnp.log(jnp.full(lse.shape, 2.0 * ROWS, jnp.float32))) / CELLS
    evidence[...] = jnp.sum(per_cell, axis=0, keepdims=True)


def on_device(
    particles, ancestors, migration, pattern, coupling, cell_rate, current, observed, noise_seeds
):
    position = lax.axis_index("island")
    half = (position % 2).astype(jnp.int32)[None]
    temper = (0.25 * jnp.power(2.0, (position // 2 % 4).astype(jnp.float32)))[None]
    shape = jax.ShapeDtypeStruct

    weights = pl.pallas_call(
        weights_kernel,
        out_shape=shape((BLOCKS, NEIGH * HALF, LANES), jnp.bfloat16),
        in_specs=[HBM],
        out_specs=VMEM,
        scratch_shapes=[
            pltpu.VMEM((NEIGH, BLOCKS, BLOCK * BLOCK), jnp.bfloat16),
            pltpu.VMEM((NEIGH, HALF * 16, LANES), jnp.float32),
            pltpu.SemaphoreType.DMA((BLOCKS // 16,)),
        ],
        compiler_params=params(10),
        cost_estimate=pl.CostEstimate(flops=3000000, bytes_accessed=10000000, transcendentals=0),
        name="weights",
    )(in_hbm(coupling.transpose(1, 0, 2)))

    ancestors, migration = in_hbm(ancestors), in_hbm(migration)
    states = particles
    logliks = ()
    rates = cell_rate.reshape(PAIRS, LANES)
    for epoch in range(EPOCHS):
        partner = from_partner(states)
        noise = pl.pallas_call(
            functools.partial(noise_kernel, epoch),
            out_shape=shape((STEPS_EPOCH, PAIRS, STATES * ROWS, LANES), jnp.float32),
            in_specs=[SMEM],
            out_specs=VMEM,
            compiler_params=params(2),
            cost_estimate=pl.CostEstimate(flops=15000000, bytes_accessed=6000000, transcendentals=0),
            name="noise",
        )(in_hbm(noise_seeds))
        partner, noise = lax.optimization_barrier((partner, noise))
        leaving = pl.pallas_call(
            functools.partial(leaving_kernel, epoch),
            out_shape=shape((1, STATES, CELLS), jnp.bfloat16),
            in_specs=[SMEM, SMEM, SMEM, HBM, HBM],
            out_specs=HBM,
            scratch_shapes=[pltpu.SemaphoreType.DMA],
            compiler_params=params(1),
            name="leaving",
        )(ancestors, migration, half, states if epoch else in_hbm(states), partner)
        arriving = from_behind(leaving)
        states, logliks = pl.pallas_call(
            functools.partial(epoch_kernel, epoch),
            out_shape=(
                shape((ROWS, STATES, CELLS), jnp.bfloat16),
                shape((EPOCHS, LANES), jnp.float32),
            ),
            in_specs=[SMEM] * 6 + [VMEM] * (8 if epoch else 7),
            out_specs=(VMEM, VMEM),
            scratch_shapes=[
                pltpu.VMEM((PAIRS, STATES * ROWS, LANES), jnp.float32),
                pltpu.VMEM((PAIRS, STATES * ROWS, LANES), jnp.bfloat16),
                pltpu.VMEM((BLOCKS, 2 * STATES * ROWS, LANES), jnp.bfloat16),
                pltpu.VMEM((BLOCKS, 2 * STATES * ROWS, LANES), jnp.bfloat16),
                pltpu.VMEM((GROUP, STATES * ROWS, LANES), jnp.float32),
                pltpu.VMEM((LANES, 4 * LANES), jnp.bfloat16),
                pltpu.VMEM((ROWS, LANES), jnp.float32),
            ],
            compiler_params=params(12),
            name="epoch",
        )(
            ancestors,
            migration,
            half,
            in_hbm(pattern.T),
            in_hbm(current),
            temper,
            states,
            partner,
            arriving,
            weights,
            noise,
            rates,
            observed,
            *([logliks] if epoch else []),
        )
    log_weight, evidence = pl.pallas_call(
        weigh_kernel,
        out_shape=(shape((EPOCHS, ROWS), jnp.float32), shape((1, 1), jnp.float32)),
        in_specs=[VMEM, VMEM],
        out_specs=(VMEM, VMEM),
        compiler_params=params(1),
        name="weigh",
    )(logliks, from_partner(logliks))
    return (states, evidence.reshape(1), log_weight)


def solution(mesh):
    return jax.shard_map(
        on_device,
        mesh=mesh,
        in_specs=(
            P(("group", "island"), None, None),
            P(None, ("group", "island"), None),
            P(None, ("group", "island"), None),
            P("group", None),
            P("group", None, None),
            P("group"),
            P("group"),
            P("group", None),
            P(("group", "island"), None),
        ),
        out_specs=(
            P(("group", "island"), None, None),
            P(("group", "island")),
            P(None, ("group", "island")),
        ),
        check_vma=False,
    )
```

```python
import functools

import jax
import jax.numpy as jnp
from jax import lax
from jax.experimental import pallas as pl
from jax.experimental.pallas import tpu as pltpu
from jax.sharding import PartitionSpec as P

CELLS = 8192
STATES = 4
BLOCK = 64
NEIGH = 5
EPOCHS = 2
STEPS_EPOCH = 2
STEPS = EPOCHS * STEPS_EPOCH
BLOCKS = 128
ROWS = 8
LANES = 128
GROUP = 16
PAIRS = CELLS // LANES
HALF = BLOCK // 2
NOISE_SCALE = 0.3 * 2.449489742783178 / 16777216.0

VMEM = pl.BlockSpec(memory_space=pltpu.VMEM)
SMEM = pl.BlockSpec(memory_space=pltpu.SMEM)
HBM = pl.BlockSpec(memory_space=pl.ANY)


def in_hbm(array):
    return pltpu.with_memory_space_constraint(array, pltpu.HBM)


def params(mib):
    return pltpu.CompilerParams(vmem_limit_bytes=mib << 20)


def from_partner(value):
    pairs = [(source, source ^ 1) for source in range(lax.axis_size("island"))]
    return lax.ppermute(value, "island", pairs)


def from_behind(block):
    count = lax.axis_size("island")
    route = [((i - 2) % count, i) for i in range(count)]
    return lax.ppermute(block, "island", route)


def shifted(hashed):
    return hashed ^ lax.shift_right_logical(hashed, jnp.full(hashed.shape, 16, jnp.int32))


def scramble(hashed):
    hashed = shifted(hashed) * 73244475
    hashed = shifted(hashed) * 73244475
    return shifted(hashed) & 16777215


def draw(step, seed, out):
    row = lax.broadcasted_iota(jnp.int32, (STATES * ROWS, LANES), 0)
    lane = lax.broadcasted_iota(jnp.int32, (STATES * ROWS, LANES), 1)
    start = 2 * (((row % ROWS) * STATES + row // ROWS) * CELLS + lane) + seed * 40503

    def one(q, carry):
        anchor = start + q * (2 * LANES)
        apart = scramble(anchor) - scramble(anchor + 1)
        out[step, q] = apart.astype(jnp.float32) * NOISE_SCALE
        return carry

    lax.fori_loop(0, PAIRS, one, 0, unroll=4)


def first_noise_kernel(*refs):
    sources, out, targets, (half, temper, sems) = refs[:5], refs[5], refs[6:11], refs[11:]
    copies = [
        pltpu.make_async_copy(source, target, sems.at[i])
        for i, (source, target) in enumerate(zip(sources, targets))
    ]
    for copy in copies:
        copy.start()
    position = lax.axis_index("island")
    half[0] = position & 1
    temper[0] = 0.25 * lax.shift_left(jnp.int32(1), (position >> 1) & 3).astype(jnp.float32)
    for copy in copies:
        copy.wait()
    for step in range(STEPS_EPOCH):
        draw(step, targets[0][0, step], out)


def noise_kernel(seeds, out):
    for step in range(STEPS_EPOCH):
        draw(step, seeds[0, STEPS_EPOCH + step], out)


def weights_kernel(coupling, out, held, wide, sems):
    group = 16

    def fetch(g):
        rows = pl.ds(pl.multiple_of(g * group, group), group)
        return pltpu.make_async_copy(coupling.at[:, rows], held.at[:, rows], sems.at[g])

    for g in range(BLOCKS // group):
        fetch(g).start()

    def one(g, carry):
        fetch(g).wait()
        for k in range(NEIGH):
            for r in range(HALF):
                wide[k, r * group : (r + 1) * group, :] = held[
                    k, pl.ds(pl.multiple_of(g * group, group), group), r * LANES : (r + 1) * LANES
                ].astype(jnp.float32)
            for b in range(group):
                picked = wide[k, pl.ds(b, HALF, stride=group), :]
                out[
                    g * (group // 2) + b // 2,
                    k * HALF : (k + 1) * HALF,
                    (b % 2) * LANES : (b % 2 + 1) * LANES,
                ] = picked.astype(jnp.bfloat16)
        return carry

    lax.fori_loop(0, BLOCKS // group, one, 0)


def leaving_kernel(epoch, ancestors, migration, half, local, partner, out, sem):
    chosen = ancestors[epoch, 0, migration[epoch, 0, 0]]
    slot = chosen % ROWS
    is_local = chosen // ROWS == half[0]

    @pl.when(is_local)
    def _():
        copy = pltpu.make_async_copy(local.at[pl.ds(slot, 1)], out, sem)
        copy.start()
        copy.wait()

    @pl.when(jnp.logical_not(is_local))
    def _():
        copy = pltpu.make_async_copy(partner.at[pl.ds(slot, 1)], out, sem)
        copy.start()
        copy.wait()


def members(g):
    return [g * GROUP + i for i in range(GROUP)]


def in_turn(*stages):
    count = PAIRS // GROUP
    depth = len(stages)

    def one(at, low, high):
        for s in reversed(range(low, high)):
            stages[s](at - s)

    def steady(at, carry):
        one(at, 0, depth)
        return carry

    for at in range(depth - 1):
        one(at, 0, at + 1)
    lax.fori_loop(depth - 1, count, steady, 0, unroll=2)
    for at in range(count, count + depth - 1):
        one(at, at - count + 1, depth)


def epoch_kernel(
    epoch,
    ancestors,
    migration,
    half,
    pattern,
    current,
    temper,
    local,
    partner,
    arriving,
    weights,
    noise,
    cell_rate,
    observed,
    *rest,
):
    if epoch:
        before, *rest = rest
    states, logliks, gather, natural, spread, spread_next, coupled, unmix, total = rest
    lane = lax.broadcasted_iota(jnp.int32, (1, LANES), 1)

    source = lax.broadcasted_iota(jnp.int32, (LANES, 4 * LANES), 0)
    target = lax.broadcasted_iota(jnp.int32, (LANES, 4 * LANES), 1)
    wanted = (target >> 8) * BLOCK + (target & (HALF - 1)) * 2 + ((target >> 7) & 1)
    unmix[...] = jnp.where(source == wanted, 1.0, 0.0).astype(jnp.bfloat16)

    picks = []
    for j in range(ROWS):
        chosen = ancestors[epoch, 0, j]
        picks.append((chosen % ROWS, chosen // ROWS == half[0], migration[epoch, 0, 0] == j))

    rows = STATES * ROWS
    total[...] = jnp.zeros_like(total)

    def assemble(g):
        for q in members(g):
            lanes = pl.ds(pl.multiple_of(q * LANES, LANES), LANES)
            for j, (slot, is_local, is_new) in enumerate(picks):
                kept = jnp.where(
                    is_local,
                    local[slot, :, lanes].astype(jnp.float32),
                    partner[slot, :, lanes].astype(jnp.float32),
                )
                gather[q, j * STATES : (j + 1) * STATES, :] = jnp.where(
                    is_new, arriving[0, :, lanes].astype(jnp.float32), kept
                )
            for c in range(0, STATES, 2):
                two = [gather[q, pl.ds(c + d, ROWS, stride=STATES), :] for d in range(2)]
                natural[q, c * ROWS : (c + 2) * ROWS, :] = jnp.concatenate(two, axis=0).astype(
                    jnp.bfloat16
                )

    def spread_out(result, g):
        cells = natural[pl.ds(g * GROUP, GROUP)].reshape(GROUP * rows, LANES)
        placed = jnp.dot(cells, unmix[...], preferred_element_type=jnp.float32).astype(jnp.bfloat16)
        for i, q in enumerate(members(g)):
            for tile in range(4):
                result[2 * q + tile // 2, (tile % 2) * rows : (tile % 2 + 1) * rows, :] = placed[
                    i * rows : (i + 1) * rows, tile * LANES : (tile + 1) * LANES
                ]

    def inputs(held, b):
        pieces = [held[pattern[k, b]] for k in range(NEIGH)]
        first = jnp.where(
            lane < HALF,
            pieces[0],
            jnp.where(lane < 2 * HALF, pieces[1], jnp.where(lane < 3 * HALF, pieces[2], pieces[3])),
        )
        return jnp.concatenate([first, pieces[4][:, :HALF]], axis=1)

    def couple(held, g):
        for i, q in enumerate(members(g)):
            both = jnp.concatenate([inputs(held, 2 * q), inputs(held, 2 * q + 1)], axis=0)
            product = jnp.dot(both, weights[q], preferred_element_type=jnp.float32)
            left, right = product[: 2 * rows, :LANES], product[2 * rows :, LANES:]
            inside = jnp.where(lane < BLOCK, left[:rows], right[rows:])
            across = jnp.where(lane < BLOCK, right[:rows], left[rows:])
            coupled[i] = inside + pltpu.roll(across, BLOCK, 1)

    def propagate(step, g):
        now = current[step]
        gained = jnp.zeros((ROWS, LANES), jnp.float32)
        for i, q in enumerate(members(g)):
            mixed = 0.6 * natural[q].astype(jnp.float32) + 0.8 * coupled[i]
            drawn = noise[step % STEPS_EPOCH, q]
            charge, over, heat, film = (mixed[c * ROWS : (c + 1) * ROWS] for c in range(STATES))
            rate = cell_rate[pl.ds(q, 1), :]
            seen = observed[step : step + 1, pl.ds(pl.multiple_of(q * LANES, LANES), LANES)]
            tanh_over = jnp.tanh(over)
            fade = jnp.exp(-0.5 * jnp.abs(charge))
            warm = 0.6 * jnp.tanh(heat)
            rise = jnp.exp(warm + 2.0 * tanh_over) - jnp.exp(warm - 2.0 * tanh_over)
            reaction = (0.5 * rate) * rise * fade / (1.0 + fade * fade)
            new_charge = charge - 0.25 * reaction + drawn[:ROWS]
            new_over = 0.7 * over + 0.5 * (now - reaction) + drawn[ROWS : 2 * ROWS]
            new_heat = 0.9 * heat + 0.2 * reaction * tanh_over + drawn[2 * ROWS : 3 * ROWS]
            new_film = 0.95 * film + 0.02 * reaction * reaction + drawn[3 * ROWS :]
            predicted = (
                0.5 + 0.5 * jnp.tanh(0.5 * new_charge) - 0.4 * jnp.tanh(new_over) - (0.2 * now) * new_film
            )
            misfit = seen - predicted
            gained += misfit * misfit
            fresh = (new_charge, new_over, new_heat, new_film)
            if step % STEPS_EPOCH == STEPS_EPOCH - 1:
                for c in range(STATES):
                    gather[q, pl.ds(c, ROWS, stride=STATES), :] = fresh[c]
            else:
                natural[q] = jnp.concatenate(fresh, axis=0).astype(jnp.bfloat16)
        total[...] += gained

    def finish(g):
        for q in members(g):
            lanes = pl.ds(pl.multiple_of(q * LANES, LANES), LANES)
            for j in range(ROWS):
                states[j, :, lanes] = gather[q, j * STATES : (j + 1) * STATES, :].astype(jnp.bfloat16)

    step = epoch * STEPS_EPOCH
    in_turn(assemble, functools.partial(spread_out, spread))
    in_turn(
        functools.partial(couple, spread),
        functools.partial(propagate, step),
        functools.partial(spread_out, spread_next),
    )
    in_turn(functools.partial(couple, spread_next), functools.partial(propagate, step + 1), finish)

    column = -0.5 * temper[0] * jnp.sum(total[...], axis=1, keepdims=True)
    slots = lax.broadcasted_iota(jnp.int32, (ROWS, LANES), 0)
    across_lanes = jnp.sum(jnp.where(slots == lane, column, 0.0), axis=0, keepdims=True)
    if epoch:
        logliks[0:1, :] = before[0:1, :]
    logliks[epoch : epoch + 1, :] = across_lanes


def weigh_kernel(own, other, log_weight, evidence):
    lane = lax.broadcasted_iota(jnp.int32, (EPOCHS, LANES), 1)
    real = lane < ROWS
    mine, theirs = own[...], other[...]
    peak = jnp.max(jnp.where(real, jnp.maximum(mine, theirs), -jnp.inf), axis=1, keepdims=True)
    shares = jnp.where(real, jnp.exp(mine - peak) + jnp.exp(theirs - peak), 0.0)
    lse = peak + jnp.log(jnp.sum(shares, axis=1, keepdims=True))
    log_weight[...] = (mine - lse)[:, :ROWS]
    per_cell = (lse - jnp.log(jnp.full(lse.shape, 2.0 * ROWS, jnp.float32))) / CELLS
    evidence[...] = jnp.sum(per_cell, axis=0, keepdims=True)


def on_device(
    particles, ancestors, migration, pattern, coupling, cell_rate, current, observed, noise_seeds
):
    shape = jax.ShapeDtypeStruct
    vector = shape((STEPS_EPOCH, PAIRS, STATES * ROWS, LANES), jnp.float32)
    cost = pl.CostEstimate(flops=15000000, bytes_accessed=6000000, transcendentals=0)
    partner = from_partner(particles)
    scalars = (noise_seeds, ancestors, migration, pattern.T, current)
    noise, *scalars = pl.pallas_call(
        first_noise_kernel,
        out_shape=(
            vector,
            *(pltpu.SMEM(x.shape, x.dtype) for x in scalars),
            pltpu.SMEM((1,), jnp.int32),
            pltpu.SMEM((1,), jnp.float32),
        ),
        in_specs=[HBM] * 5,
        out_specs=(VMEM, *[SMEM] * 7),
        scratch_shapes=[pltpu.SemaphoreType.DMA((5,))],
        compiler_params=params(2),
        cost_estimate=cost,
        name="noise",
    )(*(in_hbm(x) for x in scalars))
    seeds, ancestors, migration, pattern, current, half, temper = scalars
    weights = pl.pallas_call(
        weights_kernel,
        out_shape=shape((PAIRS, NEIGH * HALF, 2 * LANES), jnp.bfloat16),
        in_specs=[HBM],
        out_specs=VMEM,
        scratch_shapes=[
            pltpu.VMEM((NEIGH, BLOCKS, BLOCK * BLOCK), jnp.bfloat16),
            pltpu.VMEM((NEIGH, HALF * 16, LANES), jnp.float32),
            pltpu.SemaphoreType.DMA((BLOCKS // 16,)),
        ],
        compiler_params=params(10),
        cost_estimate=pl.CostEstimate(flops=3000000, bytes_accessed=10000000, transcendentals=0),
        name="weights",
    )(in_hbm(coupling.transpose(1, 0, 2)))

    states = particles
    logliks = ()
    rates = cell_rate.reshape(PAIRS, LANES)
    for epoch in range(EPOCHS):
        if epoch:
            partner = from_partner(states)
            noise = pl.pallas_call(
                noise_kernel,
                out_shape=vector,
                in_specs=[SMEM],
                out_specs=VMEM,
                compiler_params=params(2),
                cost_estimate=cost,
                name="noise",
            )(seeds)
        partner, noise = lax.optimization_barrier((partner, noise))
        leaving = pl.pallas_call(
            functools.partial(leaving_kernel, epoch),
            out_shape=shape((1, STATES, CELLS), jnp.bfloat16),
            in_specs=[SMEM, SMEM, SMEM, HBM, HBM],
            out_specs=HBM,
            scratch_shapes=[pltpu.SemaphoreType.DMA],
            compiler_params=params(1),
            name="leaving",
        )(ancestors, migration, half, states if epoch else in_hbm(states), partner)
        arriving = from_behind(leaving)
        states, logliks = pl.pallas_call(
            functools.partial(epoch_kernel, epoch),
            out_shape=(
                shape((ROWS, STATES, CELLS), jnp.bfloat16),
                shape((EPOCHS, LANES), jnp.float32),
            ),
            in_specs=[SMEM] * 6 + [VMEM] * (8 if epoch else 7),
            out_specs=(VMEM, VMEM),
            scratch_shapes=[
                pltpu.VMEM((PAIRS, STATES * ROWS, LANES), jnp.float32),
                pltpu.VMEM((PAIRS, STATES * ROWS, LANES), jnp.bfloat16),
                pltpu.VMEM((BLOCKS, 2 * STATES * ROWS, LANES), jnp.bfloat16),
                pltpu.VMEM((BLOCKS, 2 * STATES * ROWS, LANES), jnp.bfloat16),
                pltpu.VMEM((GROUP, STATES * ROWS, LANES), jnp.float32),
                pltpu.VMEM((LANES, 4 * LANES), jnp.bfloat16),
                pltpu.VMEM((ROWS, LANES), jnp.float32),
            ],
            compiler_params=params(12),
            name="epoch",
        )(
            ancestors,
            migration,
            half,
            pattern,
            current,
            temper,
            states,
            partner,
            arriving,
            weights,
            noise,
            rates,
            observed,
            *([logliks] if epoch else []),
        )
    log_weight, evidence = pl.pallas_call(
        weigh_kernel,
        out_shape=(shape((EPOCHS, ROWS), jnp.float32), shape((1, 1), jnp.float32)),
        in_specs=[VMEM, VMEM],
        out_specs=(VMEM, VMEM),
        compiler_params=params(1),
        name="weigh",
    )(logliks, from_partner(logliks))
    return (states, evidence.reshape(1), log_weight)


def solution(mesh):
    return jax.shard_map(
        on_device,
        mesh=mesh,
        in_specs=(
            P(("group", "island"), None, None),
            P(None, ("group", "island"), None),
            P(None, ("group", "island"), None),
            P("group", None),
            P("group", None, None),
            P("group"),
            P("group"),
            P("group", None),
            P(("group", "island"), None),
        ),
        out_specs=(
            P(("group", "island"), None, None),
            P(("group", "island")),
            P(None, ("group", "island")),
        ),
        check_vma=False,
    )
```

```python
import functools

import jax
import jax.numpy as jnp
from jax import lax
from jax.experimental import pallas as pl
from jax.experimental.pallas import tpu as pltpu
from jax.sharding import PartitionSpec as P

CELLS = 8192
STATES = 4
BLOCK = 64
NEIGH = 5
EPOCHS = 2
STEPS_EPOCH = 2
STEPS = EPOCHS * STEPS_EPOCH
BLOCKS = 128
ROWS = 8
LANES = 128
GROUP = 16
PAIRS = CELLS // LANES
HALF = BLOCK // 2
NOISE_SCALE = 0.3 * 2.449489742783178 / 16777216.0

VMEM = pl.BlockSpec(memory_space=pltpu.VMEM)
SMEM = pl.BlockSpec(memory_space=pltpu.SMEM)
HBM = pl.BlockSpec(memory_space=pl.ANY)


def in_hbm(array):
    return pltpu.with_memory_space_constraint(array, pltpu.HBM)


def params(mib):
    return pltpu.CompilerParams(vmem_limit_bytes=mib << 20)


def from_partner(value):
    pairs = [(source, source ^ 1) for source in range(lax.axis_size("island"))]
    return lax.ppermute(value, "island", pairs)


def from_behind(block):
    count = lax.axis_size("island")
    route = [((i - 2) % count, i) for i in range(count)]
    return lax.ppermute(block, "island", route)


def shifted(hashed):
    return hashed ^ lax.shift_right_logical(hashed, jnp.full(hashed.shape, 16, jnp.int32))


def scramble(hashed):
    hashed = shifted(hashed) * 73244475
    hashed = shifted(hashed) * 73244475
    return shifted(hashed) & 16777215


def draw(step, seed, out):
    row = lax.broadcasted_iota(jnp.int32, (STATES * ROWS, LANES), 0)
    lane = lax.broadcasted_iota(jnp.int32, (STATES * ROWS, LANES), 1)
    start = 2 * (((row % ROWS) * STATES + row // ROWS) * CELLS + lane) + seed * 40503

    def one(q, carry):
        anchor = start + q * (2 * LANES)
        apart = scramble(anchor) - scramble(anchor + 1)
        out[step, q] = apart.astype(jnp.float32) * NOISE_SCALE
        return carry

    lax.fori_loop(0, PAIRS, one, 0, unroll=4)


def first_noise_kernel(*refs):
    sources, out, targets, (half, temper, sems) = refs[:5], refs[5], refs[6:11], refs[11:]
    copies = [
        pltpu.make_async_copy(source, target, sems.at[i])
        for i, (source, target) in enumerate(zip(sources, targets))
    ]
    for copy in copies:
        copy.start()
    position = lax.axis_index("island")
    half[0] = position & 1
    temper[0] = 0.25 * lax.shift_left(jnp.int32(1), (position >> 1) & 3).astype(jnp.float32)
    for copy in copies:
        copy.wait()
    for step in range(STEPS_EPOCH):
        draw(step, targets[0][0, step], out)


def noise_kernel(seeds, out):
    for step in range(STEPS_EPOCH):
        draw(step, seeds[0, STEPS_EPOCH + step], out)


def weights_kernel(coupling, out, held, wide, sems):
    group = 16
    lane = lax.broadcasted_iota(jnp.int32, (1, LANES), 1)

    def fetch(g):
        rows = pl.ds(pl.multiple_of(g * group, group), group)
        return pltpu.make_async_copy(coupling.at[:, rows], held.at[:, rows], sems.at[g])

    for g in range(BLOCKS // group):
        fetch(g).start()

    def one(g, carry):
        fetch(g).wait()
        for k in range(NEIGH):
            for r in range(HALF):
                wide[k, r * group : (r + 1) * group, :] = held[
                    k, pl.ds(pl.multiple_of(g * group, group), group), r * LANES : (r + 1) * LANES
                ].astype(jnp.float32)
            for b in range(0, group, 2):
                left, right = (wide[k, pl.ds(b + d, HALF, stride=group), :] for d in range(2))
                across = pltpu.roll(jnp.where(lane < BLOCK, right, left), BLOCK, 1)
                even, odd = jnp.where(lane < BLOCK, left, across), jnp.where(lane < BLOCK, across, right)
                out[
                    g * (group // 4) + b // 4,
                    k * BLOCK : (k + 1) * BLOCK,
                    (b // 2 % 2) * LANES : (b // 2 % 2 + 1) * LANES,
                ] = jnp.concatenate([even, odd], axis=0).astype(jnp.bfloat16)
        return carry

    lax.fori_loop(0, BLOCKS // group, one, 0)


def leaving_kernel(epoch, ancestors, migration, half, local, partner, out, sem):
    chosen = ancestors[epoch, 0, migration[epoch, 0, 0]]
    slot = chosen % ROWS
    is_local = chosen // ROWS == half[0]

    @pl.when(is_local)
    def _():
        copy = pltpu.make_async_copy(local.at[pl.ds(slot, 1)], out, sem)
        copy.start()
        copy.wait()

    @pl.when(jnp.logical_not(is_local))
    def _():
        copy = pltpu.make_async_copy(partner.at[pl.ds(slot, 1)], out, sem)
        copy.start()
        copy.wait()


def members(g):
    return [g * GROUP + i for i in range(GROUP)]


def in_turn(*stages):
    count = PAIRS // GROUP
    depth = len(stages)

    def one(at, low, high):
        for s in reversed(range(low, high)):
            stages[s](at - s)

    def steady(at, carry):
        one(at, 0, depth)
        return carry

    for at in range(depth - 1):
        one(at, 0, at + 1)
    lax.fori_loop(depth - 1, count, steady, 0, unroll=2)
    for at in range(count, count + depth - 1):
        one(at, at - count + 1, depth)


def epoch_kernel(
    epoch,
    ancestors,
    migration,
    half,
    pattern,
    current,
    temper,
    local,
    partner,
    arriving,
    weights,
    noise,
    cell_rate,
    observed,
    *rest,
):
    if epoch:
        before, *rest = rest
    states, logliks, gather, natural, spread, spread_next, coupled, unmix, total = rest
    lane = lax.broadcasted_iota(jnp.int32, (1, LANES), 1)

    source = lax.broadcasted_iota(jnp.int32, (LANES, 2 * LANES), 0)
    target = lax.broadcasted_iota(jnp.int32, (LANES, 2 * LANES), 1)
    wanted = (target >> 7) * BLOCK + (target & (HALF - 1)) * 2 + ((target >> 5) & 1)
    unmix[...] = jnp.where(source == wanted, 1.0, 0.0).astype(jnp.bfloat16)

    picks = []
    for j in range(ROWS):
        chosen = ancestors[epoch, 0, j]
        picks.append((chosen % ROWS, chosen // ROWS == half[0], migration[epoch, 0, 0] == j))

    rows = STATES * ROWS
    total[...] = jnp.zeros_like(total)

    def assemble(g):
        for q in members(g):
            lanes = pl.ds(pl.multiple_of(q * LANES, LANES), LANES)
            for j, (slot, is_local, is_new) in enumerate(picks):
                kept = jnp.where(
                    is_local,
                    local[slot, :, lanes].astype(jnp.float32),
                    partner[slot, :, lanes].astype(jnp.float32),
                )
                gather[q, j * STATES : (j + 1) * STATES, :] = jnp.where(
                    is_new, arriving[0, :, lanes].astype(jnp.float32), kept
                )
            for c in range(0, STATES, 2):
                two = [gather[q, pl.ds(c + d, ROWS, stride=STATES), :] for d in range(2)]
                natural[q, c * ROWS : (c + 2) * ROWS, :] = jnp.concatenate(two, axis=0).astype(
                    jnp.bfloat16
                )

    def spread_out(result, g):
        cells = natural[pl.ds(g * GROUP, GROUP)].reshape(GROUP * rows, LANES)
        placed = jnp.dot(cells, unmix[...], preferred_element_type=jnp.float32).astype(jnp.bfloat16)
        for i, q in enumerate(members(g)):
            for side in range(2):
                result[2 * q + side] = placed[
                    i * rows : (i + 1) * rows, side * LANES : (side + 1) * LANES
                ]

    def inputs(held, b):
        pieces = [held[pattern[k, b]] for k in range(NEIGH)]
        return jnp.concatenate(
            [
                jnp.where(lane < BLOCK, pieces[0], pieces[1]),
                jnp.where(lane < BLOCK, pieces[2], pieces[3]),
                pieces[4][:, :BLOCK],
            ],
            axis=1,
        )

    def couple(held, g):
        for i in range(0, GROUP, 2):
            quad = g * (GROUP // 2) + i // 2
            four = jnp.concatenate([inputs(held, 4 * quad + d) for d in range(4)], axis=0)
            product = jnp.dot(four, weights[quad], preferred_element_type=jnp.float32)
            for side in range(2):
                part = product[2 * side * rows : 2 * (side + 1) * rows, side * LANES : (side + 1) * LANES]
                coupled[i + side] = jnp.where(lane < BLOCK, part[:rows], part[rows:])

    def propagate(step, g):
        now = current[step]
        gained = jnp.zeros((ROWS, LANES), jnp.float32)
        for i, q in enumerate(members(g)):
            mixed = 0.6 * natural[q].astype(jnp.float32) + 0.8 * coupled[i]
            drawn = noise[step % STEPS_EPOCH, q]
            charge, over, heat, film = (mixed[c * ROWS : (c + 1) * ROWS] for c in range(STATES))
            rate = cell_rate[pl.ds(q, 1), :]
            seen = observed[step : step + 1, pl.ds(pl.multiple_of(q * LANES, LANES), LANES)]
            tanh_over = jnp.tanh(over)
            fade = jnp.exp(-0.5 * jnp.abs(charge))
            warm = 0.6 * jnp.tanh(heat)
            rise = jnp.exp(warm + 2.0 * tanh_over) - jnp.exp(warm - 2.0 * tanh_over)
            reaction = (0.5 * rate) * rise * fade / (1.0 + fade * fade)
            new_charge = charge - 0.25 * reaction + drawn[:ROWS]
            new_over = 0.7 * over + 0.5 * (now - reaction) + drawn[ROWS : 2 * ROWS]
            new_heat = 0.9 * heat + 0.2 * reaction * tanh_over + drawn[2 * ROWS : 3 * ROWS]
            new_film = 0.95 * film + 0.02 * reaction * reaction + drawn[3 * ROWS :]
            predicted = (
                0.5 + 0.5 * jnp.tanh(0.5 * new_charge) - 0.4 * jnp.tanh(new_over) - (0.2 * now) * new_film
            )
            misfit = seen - predicted
            gained += misfit * misfit
            fresh = (new_charge, new_over, new_heat, new_film)
            if step % STEPS_EPOCH == STEPS_EPOCH - 1:
                for c in range(STATES):
                    gather[q, pl.ds(c, ROWS, stride=STATES), :] = fresh[c]
            else:
                natural[q] = jnp.concatenate(fresh, axis=0).astype(jnp.bfloat16)
        total[...] += gained

    def finish(g):
        for q in members(g):
            lanes = pl.ds(pl.multiple_of(q * LANES, LANES), LANES)
            for j in range(ROWS):
                states[j, :, lanes] = gather[q, j * STATES : (j + 1) * STATES, :].astype(jnp.bfloat16)

    step = epoch * STEPS_EPOCH
    in_turn(assemble, functools.partial(spread_out, spread))
    in_turn(
        functools.partial(couple, spread),
        functools.partial(propagate, step),
        functools.partial(spread_out, spread_next),
    )
    in_turn(functools.partial(couple, spread_next), functools.partial(propagate, step + 1), finish)

    column = -0.5 * temper[0] * jnp.sum(total[...], axis=1, keepdims=True)
    slots = lax.broadcasted_iota(jnp.int32, (ROWS, LANES), 0)
    across_lanes = jnp.sum(jnp.where(slots == lane, column, 0.0), axis=0, keepdims=True)
    if epoch:
        logliks[0:1, :] = before[0:1, :]
    logliks[epoch : epoch + 1, :] = across_lanes


def weigh_kernel(own, other, log_weight, evidence):
    lane = lax.broadcasted_iota(jnp.int32, (EPOCHS, LANES), 1)
    real = lane < ROWS
    mine, theirs = own[...], other[...]
    peak = jnp.max(jnp.where(real, jnp.maximum(mine, theirs), -jnp.inf), axis=1, keepdims=True)
    shares = jnp.where(real, jnp.exp(mine - peak) + jnp.exp(theirs - peak), 0.0)
    lse = peak + jnp.log(jnp.sum(shares, axis=1, keepdims=True))
    log_weight[...] = (mine - lse)[:, :ROWS]
    per_cell = (lse - jnp.log(jnp.full(lse.shape, 2.0 * ROWS, jnp.float32))) / CELLS
    evidence[...] = jnp.sum(per_cell, axis=0, keepdims=True)


def on_device(
    particles, ancestors, migration, pattern, coupling, cell_rate, current, observed, noise_seeds
):
    shape = jax.ShapeDtypeStruct
    vector = shape((STEPS_EPOCH, PAIRS, STATES * ROWS, LANES), jnp.float32)
    cost = pl.CostEstimate(flops=15000000, bytes_accessed=6000000, transcendentals=0)
    partner = from_partner(particles)
    scalars = (noise_seeds, ancestors, migration, pattern.T, current)
    noise, *scalars = pl.pallas_call(
        first_noise_kernel,
        out_shape=(
            vector,
            *(pltpu.SMEM(x.shape, x.dtype) for x in scalars),
            pltpu.SMEM((1,), jnp.int32),
            pltpu.SMEM((1,), jnp.float32),
        ),
        in_specs=[HBM] * 5,
        out_specs=(VMEM, *[SMEM] * 7),
        scratch_shapes=[pltpu.SemaphoreType.DMA((5,))],
        compiler_params=params(2),
        cost_estimate=cost,
        name="noise",
    )(*(in_hbm(x) for x in scalars))
    seeds, ancestors, migration, pattern, current, half, temper = scalars
    weights = pl.pallas_call(
        weights_kernel,
        out_shape=shape((BLOCKS // 4, NEIGH * BLOCK, 4 * BLOCK), jnp.bfloat16),
        in_specs=[HBM],
        out_specs=VMEM,
        scratch_shapes=[
            pltpu.VMEM((NEIGH, BLOCKS, BLOCK * BLOCK), jnp.bfloat16),
            pltpu.VMEM((NEIGH, HALF * 16, LANES), jnp.float32),
            pltpu.SemaphoreType.DMA((BLOCKS // 16,)),
        ],
        compiler_params=params(10),
        cost_estimate=pl.CostEstimate(flops=3000000, bytes_accessed=10000000, transcendentals=0),
        name="weights",
    )(in_hbm(coupling.transpose(1, 0, 2)))

    states = particles
    logliks = ()
    rates = cell_rate.reshape(PAIRS, LANES)
    for epoch in range(EPOCHS):
        if epoch:
            partner = from_partner(states)
            noise = pl.pallas_call(
                noise_kernel,
                out_shape=vector,
                in_specs=[SMEM],
                out_specs=VMEM,
                compiler_params=params(2),
                cost_estimate=cost,
                name="noise",
            )(seeds)
        partner, noise = lax.optimization_barrier((partner, noise))
        leaving = pl.pallas_call(
            functools.partial(leaving_kernel, epoch),
            out_shape=shape((1, STATES, CELLS), jnp.bfloat16),
            in_specs=[SMEM, SMEM, SMEM, HBM, HBM],
            out_specs=HBM,
            scratch_shapes=[pltpu.SemaphoreType.DMA],
            compiler_params=params(1),
            name="leaving",
        )(ancestors, migration, half, states if epoch else in_hbm(states), partner)
        arriving = from_behind(leaving)
        states, logliks = pl.pallas_call(
            functools.partial(epoch_kernel, epoch),
            out_shape=(
                shape((ROWS, STATES, CELLS), jnp.bfloat16),
                shape((EPOCHS, LANES), jnp.float32),
            ),
            in_specs=[SMEM] * 6 + [VMEM] * (8 if epoch else 7),
            out_specs=(VMEM, VMEM),
            scratch_shapes=[
                pltpu.VMEM((PAIRS, STATES * ROWS, LANES), jnp.float32),
                pltpu.VMEM((PAIRS, STATES * ROWS, LANES), jnp.bfloat16),
                pltpu.VMEM((BLOCKS, STATES * ROWS, LANES), jnp.bfloat16),
                pltpu.VMEM((BLOCKS, STATES * ROWS, LANES), jnp.bfloat16),
                pltpu.VMEM((GROUP, STATES * ROWS, LANES), jnp.float32),
                pltpu.VMEM((LANES, 2 * LANES), jnp.bfloat16),
                pltpu.VMEM((ROWS, LANES), jnp.float32),
            ],
            compiler_params=params(12),
            name="epoch",
        )(
            ancestors,
            migration,
            half,
            pattern,
            current,
            temper,
            states,
            partner,
            arriving,
            weights,
            noise,
            rates,
            observed,
            *([logliks] if epoch else []),
        )
    log_weight, evidence = pl.pallas_call(
        weigh_kernel,
        out_shape=(shape((EPOCHS, ROWS), jnp.float32), shape((1, 1), jnp.float32)),
        in_specs=[VMEM, VMEM],
        out_specs=(VMEM, VMEM),
        compiler_params=params(1),
        name="weigh",
    )(logliks, from_partner(logliks))
    return (states, evidence.reshape(1), log_weight)


def solution(mesh):
    return jax.shard_map(
        on_device,
        mesh=mesh,
        in_specs=(
            P(("group", "island"), None, None),
            P(None, ("group", "island"), None),
            P(None, ("group", "island"), None),
            P("group", None),
            P("group", None, None),
            P("group"),
            P("group"),
            P("group", None),
            P(("group", "island"), None),
        ),
        out_specs=(
            P(("group", "island"), None, None),
            P(("group", "island")),
            P(None, ("group", "island")),
        ),
        check_vma=False,
    )
```

```python
import functools

import jax
import jax.numpy as jnp
from jax import lax
from jax.experimental import pallas as pl
from jax.experimental.pallas import tpu as pltpu
from jax.sharding import PartitionSpec as P

CELLS = 8192
STATES = 4
BLOCK = 64
NEIGH = 5
EPOCHS = 2
STEPS_EPOCH = 2
STEPS = EPOCHS * STEPS_EPOCH
BLOCKS = 128
ROWS = 8
LANES = 128
TURNS = 2
GROUP = 16
PAIRS = CELLS // LANES
HALF = BLOCK // 2
NOISE_SCALE = 0.3 * 2.449489742783178 / 16777216.0

VMEM = pl.BlockSpec(memory_space=pltpu.VMEM)
SMEM = pl.BlockSpec(memory_space=pltpu.SMEM)
HBM = pl.BlockSpec(memory_space=pl.ANY)


def in_hbm(array):
    return pltpu.with_memory_space_constraint(array, pltpu.HBM)


def params(mib):
    return pltpu.CompilerParams(vmem_limit_bytes=mib << 20)


def from_partner(value):
    pairs = [(source, source ^ 1) for source in range(lax.axis_size("island"))]
    return lax.ppermute(value, "island", pairs)


def from_behind(block):
    count = lax.axis_size("island")
    route = [((i - 2) % count, i) for i in range(count)]
    return lax.ppermute(block, "island", route)


def shifted(hashed):
    return hashed ^ lax.shift_right_logical(hashed, jnp.full(hashed.shape, 16, jnp.int32))


def scramble(hashed):
    hashed = shifted(hashed) * 73244475
    hashed = shifted(hashed) * 73244475
    return shifted(hashed) & 16777215


def draw(step, seed, out):
    row = lax.broadcasted_iota(jnp.int32, (STATES * ROWS, LANES), 0)
    lane = lax.broadcasted_iota(jnp.int32, (STATES * ROWS, LANES), 1)
    start = 2 * (((row % ROWS) * STATES + row // ROWS) * CELLS + lane) + seed * 40503

    def one(q, carry):
        anchor = start + q * (2 * LANES)
        apart = scramble(anchor) - scramble(anchor + 1)
        out[step, q] = apart.astype(jnp.float32) * NOISE_SCALE
        return carry

    lax.fori_loop(0, PAIRS, one, 0, unroll=4)


def first_kernel(*refs):
    sources, out, targets, (half, temper, sems) = refs[:7], refs[7], refs[8:15], refs[15:]
    copies = [
        pltpu.make_async_copy(source, target, sems.at[i])
        for i, (source, target) in enumerate(zip(sources, targets))
    ]
    for copy in copies:
        copy.start()
    position = lax.axis_index("island")
    half[0] = position & 1
    temper[0] = 0.25 * lax.shift_left(jnp.int32(1), (position >> 1) & 3).astype(jnp.float32)
    for copy in copies[:5]:
        copy.wait()
    for step in range(STEPS_EPOCH):
        draw(step, targets[0][0, step], out)
    for copy in copies[5:]:
        copy.wait()


def noise_kernel(seeds, out):
    for step in range(STEPS_EPOCH):
        draw(step, seeds[0, STEPS_EPOCH + step], out)


def weights_kernel(coupling, out, wide):
    group = 16
    lane = lax.broadcasted_iota(jnp.int32, (1, LANES), 1)

    def move(g, k, held):
        for r in range(HALF):
            wide[held, r * group : (r + 1) * group, :] = coupling[
                k, pl.ds(pl.multiple_of(g * group, group), group), r * LANES : (r + 1) * LANES
            ].astype(jnp.float32)
        for b in range(0, group, 2):
            left, right = (wide[held, pl.ds(b + d, HALF, stride=group), :] for d in range(2))
            across = pltpu.roll(jnp.where(lane < BLOCK, right, left), BLOCK, 1)
            even, odd = jnp.where(lane < BLOCK, left, across), jnp.where(lane < BLOCK, across, right)
            out[
                g * (group // 4) + b // 4,
                k * BLOCK : (k + 1) * BLOCK,
                (b // 2 % 2) * LANES : (b // 2 % 2 + 1) * LANES,
            ] = jnp.concatenate([even, odd], axis=0).astype(jnp.bfloat16)

    def one(at, carry):
        for d in range(TURNS):
            for k in range(NEIGH):
                move(TURNS * at + d, k, d * NEIGH + k)
        return carry

    lax.fori_loop(0, BLOCKS // group // TURNS, one, 0)


def leaving_kernel(epoch, ancestors, migration, half, local, partner, out, sem):
    chosen = ancestors[epoch, 0, migration[epoch, 0, 0]]
    slot = chosen % ROWS
    is_local = chosen // ROWS == half[0]

    @pl.when(is_local)
    def _():
        copy = pltpu.make_async_copy(local.at[pl.ds(slot, 1)], out, sem)
        copy.start()
        copy.wait()

    @pl.when(jnp.logical_not(is_local))
    def _():
        copy = pltpu.make_async_copy(partner.at[pl.ds(slot, 1)], out, sem)
        copy.start()
        copy.wait()


def members(g):
    return [g * GROUP + i for i in range(GROUP)]


def in_turn(*stages):
    count = PAIRS // GROUP
    depth = len(stages)

    def one(at, low, high):
        for s in reversed(range(low, high)):
            stages[s](at - s)

    def steady(at, carry):
        one(at, 0, depth)
        return carry

    for at in range(depth - 1):
        one(at, 0, at + 1)
    lax.fori_loop(depth - 1, count, steady, 0, unroll=2)
    for at in range(count, count + depth - 1):
        one(at, at - count + 1, depth)


def epoch_kernel(
    epoch,
    ancestors,
    migration,
    half,
    pattern,
    current,
    temper,
    local,
    partner,
    arriving,
    weights,
    noise,
    cell_rate,
    observed,
    *rest,
):
    if epoch:
        before, *rest = rest
    states, logliks, gather, natural, spread, spread_next, coupled, unmix, total = rest
    lane = lax.broadcasted_iota(jnp.int32, (1, LANES), 1)

    source = lax.broadcasted_iota(jnp.int32, (LANES, 2 * LANES), 0)
    target = lax.broadcasted_iota(jnp.int32, (LANES, 2 * LANES), 1)
    wanted = (target >> 7) * BLOCK + (target & (HALF - 1)) * 2 + ((target >> 5) & 1)
    unmix[...] = jnp.where(source == wanted, 1.0, 0.0).astype(jnp.bfloat16)

    picks = []
    for j in range(ROWS):
        chosen = ancestors[epoch, 0, j]
        picks.append((chosen % ROWS, chosen // ROWS == half[0], migration[epoch, 0, 0] == j))

    rows = STATES * ROWS
    total[...] = jnp.zeros_like(total)

    def assemble(g):
        for q in members(g):
            lanes = pl.ds(pl.multiple_of(q * LANES, LANES), LANES)
            for j, (slot, is_local, is_new) in enumerate(picks):
                kept = jnp.where(
                    is_local,
                    local[slot, :, lanes].astype(jnp.float32),
                    partner[slot, :, lanes].astype(jnp.float32),
                )
                gather[q, j * STATES : (j + 1) * STATES, :] = jnp.where(
                    is_new, arriving[0, :, lanes].astype(jnp.float32), kept
                )
            for c in range(0, STATES, 2):
                two = [gather[q, pl.ds(c + d, ROWS, stride=STATES), :] for d in range(2)]
                natural[q, c * ROWS : (c + 2) * ROWS, :] = jnp.concatenate(two, axis=0).astype(
                    jnp.bfloat16
                )

    def spread_out(result, g):
        cells = natural[pl.ds(g * GROUP, GROUP)].reshape(GROUP * rows, LANES)
        placed = jnp.dot(cells, unmix[...], preferred_element_type=jnp.float32).astype(jnp.bfloat16)
        for i, q in enumerate(members(g)):
            for side in range(2):
                result[2 * q + side] = placed[
                    i * rows : (i + 1) * rows, side * LANES : (side + 1) * LANES
                ]

    def inputs(held, b):
        pieces = [held[pattern[k, b]] for k in range(NEIGH)]
        return jnp.concatenate(
            [
                jnp.where(lane < BLOCK, pieces[0], pieces[1]),
                jnp.where(lane < BLOCK, pieces[2], pieces[3]),
                pieces[4][:, :BLOCK],
            ],
            axis=1,
        )

    def couple(held, g):
        for i in range(0, GROUP, 2):
            quad = g * (GROUP // 2) + i // 2
            four = jnp.concatenate([inputs(held, 4 * quad + d) for d in range(4)], axis=0)
            product = jnp.dot(four, weights[quad], preferred_element_type=jnp.float32)
            for side in range(2):
                part = product[2 * side * rows : 2 * (side + 1) * rows, side * LANES : (side + 1) * LANES]
                coupled[i + side] = jnp.where(lane < BLOCK, part[:rows], part[rows:])

    def propagate(step, g):
        now = current[step]
        gained = jnp.zeros((ROWS, LANES), jnp.float32)
        for i, q in enumerate(members(g)):
            mixed = 0.6 * natural[q].astype(jnp.float32) + 0.8 * coupled[i]
            drawn = noise[step % STEPS_EPOCH, q]
            charge, over, heat, film = (mixed[c * ROWS : (c + 1) * ROWS] for c in range(STATES))
            rate = cell_rate[pl.ds(q, 1), :]
            seen = observed[step : step + 1, pl.ds(pl.multiple_of(q * LANES, LANES), LANES)]
            tanh_over = jnp.tanh(over)
            fade = jnp.exp(-0.5 * jnp.abs(charge))
            warm = 0.6 * jnp.tanh(heat)
            rise = jnp.exp(warm + 2.0 * tanh_over) - jnp.exp(warm - 2.0 * tanh_over)
            reaction = (0.5 * rate) * rise * fade / (1.0 + fade * fade)
            new_charge = charge - 0.25 * reaction + drawn[:ROWS]
            new_over = 0.7 * over + 0.5 * (now - reaction) + drawn[ROWS : 2 * ROWS]
            new_heat = 0.9 * heat + 0.2 * reaction * tanh_over + drawn[2 * ROWS : 3 * ROWS]
            new_film = 0.95 * film + 0.02 * reaction * reaction + drawn[3 * ROWS :]
            predicted = (
                0.5 + 0.5 * jnp.tanh(0.5 * new_charge) - 0.4 * jnp.tanh(new_over) - (0.2 * now) * new_film
            )
            misfit = seen - predicted
            gained += misfit * misfit
            fresh = (new_charge, new_over, new_heat, new_film)
            if step % STEPS_EPOCH == STEPS_EPOCH - 1:
                for c in range(STATES):
                    gather[q, pl.ds(c, ROWS, stride=STATES), :] = fresh[c]
            else:
                natural[q] = jnp.concatenate(fresh, axis=0).astype(jnp.bfloat16)
        total[...] += gained

    def finish(g):
        for q in members(g):
            lanes = pl.ds(pl.multiple_of(q * LANES, LANES), LANES)
            for j in range(ROWS):
                states[j, :, lanes] = gather[q, j * STATES : (j + 1) * STATES, :].astype(jnp.bfloat16)

    step = epoch * STEPS_EPOCH
    in_turn(assemble, functools.partial(spread_out, spread))
    in_turn(
        functools.partial(couple, spread),
        functools.partial(propagate, step),
        functools.partial(spread_out, spread_next),
    )
    in_turn(functools.partial(couple, spread_next), functools.partial(propagate, step + 1), finish)

    column = -0.5 * temper[0] * jnp.sum(total[...], axis=1, keepdims=True)
    slots = lax.broadcasted_iota(jnp.int32, (ROWS, LANES), 0)
    across_lanes = jnp.sum(jnp.where(slots == lane, column, 0.0), axis=0, keepdims=True)
    if epoch:
        logliks[0:1, :] = before[0:1, :]
    logliks[epoch : epoch + 1, :] = across_lanes


def weigh_kernel(own, other, log_weight, evidence):
    lane = lax.broadcasted_iota(jnp.int32, (EPOCHS, LANES), 1)
    real = lane < ROWS
    mine, theirs = own[...], other[...]
    peak = jnp.max(jnp.where(real, jnp.maximum(mine, theirs), -jnp.inf), axis=1, keepdims=True)
    shares = jnp.where(real, jnp.exp(mine - peak) + jnp.exp(theirs - peak), 0.0)
    lse = peak + jnp.log(jnp.sum(shares, axis=1, keepdims=True))
    log_weight[...] = (mine - lse)[:, :ROWS]
    per_cell = (lse - jnp.log(jnp.full(lse.shape, 2.0 * ROWS, jnp.float32))) / CELLS
    evidence[...] = jnp.sum(per_cell, axis=0, keepdims=True)


def on_device(
    particles, ancestors, migration, pattern, coupling, cell_rate, current, observed, noise_seeds
):
    shape = jax.ShapeDtypeStruct
    vector = shape((STEPS_EPOCH, PAIRS, STATES * ROWS, LANES), jnp.float32)
    cost = pl.CostEstimate(flops=15000000, bytes_accessed=6000000, transcendentals=0)
    partner = from_partner(particles)
    sources = (noise_seeds, ancestors, migration, pattern.T, current, particles, coupling.transpose(1, 0, 2))
    noise, seeds, ancestors, migration, pattern, current, states, coupling, half, temper = pl.pallas_call(
        first_kernel,
        out_shape=(
            vector,
            *(pltpu.SMEM(x.shape, x.dtype) for x in sources[:5]),
            *(shape(x.shape, x.dtype) for x in sources[5:]),
            pltpu.SMEM((1,), jnp.int32),
            pltpu.SMEM((1,), jnp.float32),
        ),
        in_specs=[HBM] * 7,
        out_specs=(VMEM, *[SMEM] * 5, VMEM, VMEM, SMEM, SMEM),
        scratch_shapes=[pltpu.SemaphoreType.DMA((7,))],
        compiler_params=params(2),
        cost_estimate=cost,
        name="first",
    )(*(in_hbm(x) for x in sources))
    weights = pl.pallas_call(
        weights_kernel,
        out_shape=shape((BLOCKS // 4, NEIGH * BLOCK, 4 * BLOCK), jnp.bfloat16),
        in_specs=[VMEM],
        out_specs=VMEM,
        scratch_shapes=[pltpu.VMEM((TURNS * NEIGH, HALF * 16, LANES), jnp.float32)],
        compiler_params=params(6),
        cost_estimate=pl.CostEstimate(flops=3000000, bytes_accessed=10000000, transcendentals=0),
        name="weights",
    )(coupling)

    logliks = ()
    rates = cell_rate.reshape(PAIRS, LANES)
    for epoch in range(EPOCHS):
        if epoch:
            partner = from_partner(states)
            noise = pl.pallas_call(
                noise_kernel,
                out_shape=vector,
                in_specs=[SMEM],
                out_specs=VMEM,
                compiler_params=params(2),
                cost_estimate=cost,
                name="noise",
            )(seeds)
        partner, noise = lax.optimization_barrier((partner, noise))
        leaving = pl.pallas_call(
            functools.partial(leaving_kernel, epoch),
            out_shape=shape((1, STATES, CELLS), jnp.bfloat16),
            in_specs=[SMEM, SMEM, SMEM, HBM, HBM],
            out_specs=HBM,
            scratch_shapes=[pltpu.SemaphoreType.DMA],
            compiler_params=params(1),
            name="leaving",
        )(ancestors, migration, half, states, partner)
        arriving = from_behind(leaving)
        states, logliks = pl.pallas_call(
            functools.partial(epoch_kernel, epoch),
            out_shape=(
                shape((ROWS, STATES, CELLS), jnp.bfloat16),
                shape((EPOCHS, LANES), jnp.float32),
            ),
            in_specs=[SMEM] * 6 + [VMEM] * (8 if epoch else 7),
            out_specs=(VMEM, VMEM),
            scratch_shapes=[
                pltpu.VMEM((PAIRS, STATES * ROWS, LANES), jnp.float32),
                pltpu.VMEM((PAIRS, STATES * ROWS, LANES), jnp.bfloat16),
                pltpu.VMEM((BLOCKS, STATES * ROWS, LANES), jnp.bfloat16),
                pltpu.VMEM((BLOCKS, STATES * ROWS, LANES), jnp.bfloat16),
                pltpu.VMEM((GROUP, STATES * ROWS, LANES), jnp.float32),
                pltpu.VMEM((LANES, 2 * LANES), jnp.bfloat16),
                pltpu.VMEM((ROWS, LANES), jnp.float32),
            ],
            compiler_params=params(12),
            name="epoch",
        )(
            ancestors,
            migration,
            half,
            pattern,
            current,
            temper,
            states,
            partner,
            arriving,
            weights,
            noise,
            rates,
            observed,
            *([logliks] if epoch else []),
        )
    log_weight, evidence = pl.pallas_call(
        weigh_kernel,
        out_shape=(shape((EPOCHS, ROWS), jnp.float32), shape((1, 1), jnp.float32)),
        in_specs=[VMEM, VMEM],
        out_specs=(VMEM, VMEM),
        compiler_params=params(1),
        name="weigh",
    )(logliks, from_partner(logliks))
    return (states, evidence.reshape(1), log_weight)


def solution(mesh):
    return jax.shard_map(
        on_device,
        mesh=mesh,
        in_specs=(
            P(("group", "island"), None, None),
            P(None, ("group", "island"), None),
            P(None, ("group", "island"), None),
            P("group", None),
            P("group", None, None),
            P("group"),
            P("group"),
            P("group", None),
            P(("group", "island"), None),
        ),
        out_specs=(
            P(("group", "island"), None, None),
            P(("group", "island")),
            P(None, ("group", "island")),
        ),
        check_vma=False,
    )
```

```python
import functools

import jax
import jax.numpy as jnp
from jax import lax
from jax.experimental import pallas as pl
from jax.experimental.pallas import tpu as pltpu
from jax.sharding import PartitionSpec as P

CELLS = 8192
STATES = 4
BLOCK = 64
NEIGH = 5
EPOCHS = 2
STEPS_EPOCH = 2
STEPS = EPOCHS * STEPS_EPOCH
BLOCKS = 128
ROWS = 8
LANES = 128
TURNS = 2
GROUP = 16
PAIRS = CELLS // LANES
HALF = BLOCK // 2
NOISE_SCALE = 0.3 * 2.449489742783178 / 16777216.0

VMEM = pl.BlockSpec(memory_space=pltpu.VMEM)
SMEM = pl.BlockSpec(memory_space=pltpu.SMEM)
HBM = pl.BlockSpec(memory_space=pl.ANY)


def in_hbm(array):
    return pltpu.with_memory_space_constraint(array, pltpu.HBM)


def params(mib):
    return pltpu.CompilerParams(vmem_limit_bytes=mib << 20)


def from_partner(value):
    pairs = [(source, source ^ 1) for source in range(lax.axis_size("island"))]
    return lax.ppermute(value, "island", pairs)


def from_behind(block):
    count = lax.axis_size("island")
    route = [((i - 2) % count, i) for i in range(count)]
    return lax.ppermute(block, "island", route)


def shifted(hashed):
    return hashed ^ lax.shift_right_logical(hashed, jnp.full(hashed.shape, 16, jnp.int32))


def scramble(hashed):
    hashed = shifted(hashed) * 73244475
    hashed = shifted(hashed) * 73244475
    return shifted(hashed) & 16777215


def draw(seed, out):
    row = lax.broadcasted_iota(jnp.int32, (STATES * ROWS, LANES), 0)
    lane = lax.broadcasted_iota(jnp.int32, (STATES * ROWS, LANES), 1)
    start = 2 * (((row % ROWS) * STATES + row // ROWS) * CELLS + lane) + seed * 40503

    def one(q, carry):
        anchor = start + q * (2 * LANES)
        apart = scramble(anchor) - scramble(anchor + 1)
        out[q] = apart.astype(jnp.float32) * NOISE_SCALE
        return carry

    lax.fori_loop(0, PAIRS, one, 0, unroll=4)


def first_kernel(*refs):
    sources, out, targets, (half, temper, sems) = refs[:7], refs[7], refs[8:15], refs[15:]
    sources = (*sources[:6], sources[6].at[:, : BLOCKS // 2])
    copies = [
        pltpu.make_async_copy(source, target, sems.at[i])
        for i, (source, target) in enumerate(zip(sources, targets))
    ]
    for copy in copies:
        copy.start()
    position = lax.axis_index("island")
    half[0] = position & 1
    temper[0] = 0.25 * lax.shift_left(jnp.int32(1), (position >> 1) & 3).astype(jnp.float32)
    for copy in copies[:5]:
        copy.wait()
    draw(targets[0][0, 0], out)
    for copy in copies[5:]:
        copy.wait()


def second_kernel(seeds, coupling, out, target, sem):
    copy = pltpu.make_async_copy(coupling.at[:, BLOCKS // 2 :], target, sem)
    copy.start()
    draw(seeds[0, 1], out)
    copy.wait()


def noise_kernel(seeds, *outs):
    for step, out in enumerate(outs):
        draw(seeds[0, STEPS_EPOCH + step], out)


def weights_kernel(front, back, out, wide):
    group = 16
    lane = lax.broadcasted_iota(jnp.int32, (1, LANES), 1)

    def move(coupling, g, local_g, k, held):
        for r in range(HALF):
            wide[held, r * group : (r + 1) * group, :] = coupling[
                k, pl.ds(pl.multiple_of(local_g * group, group), group), r * LANES : (r + 1) * LANES
            ].astype(jnp.float32)
        for b in range(0, group, 2):
            left, right = (wide[held, pl.ds(b + d, HALF, stride=group), :] for d in range(2))
            across = pltpu.roll(jnp.where(lane < BLOCK, right, left), BLOCK, 1)
            even, odd = jnp.where(lane < BLOCK, left, across), jnp.where(lane < BLOCK, across, right)
            out[
                g * (group // 4) + b // 4,
                k * BLOCK : (k + 1) * BLOCK,
                (b // 2 % 2) * LANES : (b // 2 % 2 + 1) * LANES,
            ] = jnp.concatenate([even, odd], axis=0).astype(jnp.bfloat16)

    groups = BLOCKS // 2 // group
    for part, coupling in enumerate((front, back)):

        def one(at, carry, part=part, coupling=coupling):
            for d in range(TURNS):
                g = TURNS * at + d
                for k in range(NEIGH):
                    move(coupling, part * groups + g, g, k, d * NEIGH + k)
            return carry

        lax.fori_loop(0, groups // TURNS, one, 0)


def leaving_kernel(epoch, ancestors, migration, half, local, partner, out, sem):
    chosen = ancestors[epoch, 0, migration[epoch, 0, 0]]
    slot = chosen % ROWS
    is_local = chosen // ROWS == half[0]

    @pl.when(is_local)
    def _():
        copy = pltpu.make_async_copy(local.at[pl.ds(slot, 1)], out, sem)
        copy.start()
        copy.wait()

    @pl.when(jnp.logical_not(is_local))
    def _():
        copy = pltpu.make_async_copy(partner.at[pl.ds(slot, 1)], out, sem)
        copy.start()
        copy.wait()


def members(g):
    return [g * GROUP + i for i in range(GROUP)]


def in_turn(*stages):
    count = PAIRS // GROUP
    depth = len(stages)

    def one(at, low, high):
        for s in reversed(range(low, high)):
            stages[s](at - s)

    def steady(at, carry):
        one(at, 0, depth)
        return carry

    for at in range(depth - 1):
        one(at, 0, at + 1)
    lax.fori_loop(depth - 1, count, steady, 0, unroll=2)
    for at in range(count, count + depth - 1):
        one(at, at - count + 1, depth)


def epoch_kernel(
    epoch,
    ancestors,
    migration,
    half,
    pattern,
    current,
    temper,
    local,
    partner,
    arriving,
    weights,
    noise_first,
    noise_second,
    cell_rate,
    observed,
    *rest,
):
    if epoch:
        before, *rest = rest
    states, logliks, gather, natural, spread, spread_next, coupled, unmix, total = rest
    lane = lax.broadcasted_iota(jnp.int32, (1, LANES), 1)

    source = lax.broadcasted_iota(jnp.int32, (LANES, 2 * LANES), 0)
    target = lax.broadcasted_iota(jnp.int32, (LANES, 2 * LANES), 1)
    wanted = (target >> 7) * BLOCK + (target & (HALF - 1)) * 2 + ((target >> 5) & 1)
    unmix[...] = jnp.where(source == wanted, 1.0, 0.0).astype(jnp.bfloat16)

    picks = []
    for j in range(ROWS):
        chosen = ancestors[epoch, 0, j]
        picks.append((chosen % ROWS, chosen // ROWS == half[0], migration[epoch, 0, 0] == j))

    rows = STATES * ROWS
    total[...] = jnp.zeros_like(total)

    def assemble(g):
        for q in members(g):
            lanes = pl.ds(pl.multiple_of(q * LANES, LANES), LANES)
            for j, (slot, is_local, is_new) in enumerate(picks):
                kept = jnp.where(
                    is_local,
                    local[slot, :, lanes].astype(jnp.float32),
                    partner[slot, :, lanes].astype(jnp.float32),
                )
                gather[q, j * STATES : (j + 1) * STATES, :] = jnp.where(
                    is_new, arriving[0, :, lanes].astype(jnp.float32), kept
                )
            for c in range(0, STATES, 2):
                two = [gather[q, pl.ds(c + d, ROWS, stride=STATES), :] for d in range(2)]
                natural[q, c * ROWS : (c + 2) * ROWS, :] = jnp.concatenate(two, axis=0).astype(
                    jnp.bfloat16
                )

    def spread_out(result, g):
        cells = natural[pl.ds(g * GROUP, GROUP)].reshape(GROUP * rows, LANES)
        placed = jnp.dot(cells, unmix[...], preferred_element_type=jnp.float32).astype(jnp.bfloat16)
        for i, q in enumerate(members(g)):
            for side in range(2):
                result[2 * q + side] = placed[
                    i * rows : (i + 1) * rows, side * LANES : (side + 1) * LANES
                ]

    def inputs(held, b):
        pieces = [held[pattern[k, b]] for k in range(NEIGH)]
        return jnp.concatenate(
            [
                jnp.where(lane < BLOCK, pieces[0], pieces[1]),
                jnp.where(lane < BLOCK, pieces[2], pieces[3]),
                pieces[4][:, :BLOCK],
            ],
            axis=1,
        )

    def couple(held, g):
        for i in range(0, GROUP, 2):
            quad = g * (GROUP // 2) + i // 2
            four = jnp.concatenate([inputs(held, 4 * quad + d) for d in range(4)], axis=0)
            product = jnp.dot(four, weights[quad], preferred_element_type=jnp.float32)
            for side in range(2):
                part = product[2 * side * rows : 2 * (side + 1) * rows, side * LANES : (side + 1) * LANES]
                coupled[i + side] = jnp.where(lane < BLOCK, part[:rows], part[rows:])

    def propagate(step, g):
        now = current[step]
        gained = jnp.zeros((ROWS, LANES), jnp.float32)
        for i, q in enumerate(members(g)):
            mixed = 0.6 * natural[q].astype(jnp.float32) + 0.8 * coupled[i]
            drawn = (noise_first, noise_second)[step % STEPS_EPOCH][q]
            charge, over, heat, film = (mixed[c * ROWS : (c + 1) * ROWS] for c in range(STATES))
            rate = cell_rate[pl.ds(q, 1), :]
            seen = observed[step : step + 1, pl.ds(pl.multiple_of(q * LANES, LANES), LANES)]
            tanh_over = jnp.tanh(over)
            fade = jnp.exp(-0.5 * jnp.abs(charge))
            warm = 0.6 * jnp.tanh(heat)
            rise = jnp.exp(warm + 2.0 * tanh_over) - jnp.exp(warm - 2.0 * tanh_over)
            reaction = (0.5 * rate) * rise * fade / (1.0 + fade * fade)
            new_charge = charge - 0.25 * reaction + drawn[:ROWS]
            new_over = 0.7 * over + 0.5 * (now - reaction) + drawn[ROWS : 2 * ROWS]
            new_heat = 0.9 * heat + 0.2 * reaction * tanh_over + drawn[2 * ROWS : 3 * ROWS]
            new_film = 0.95 * film + 0.02 * reaction * reaction + drawn[3 * ROWS :]
            predicted = (
                0.5 + 0.5 * jnp.tanh(0.5 * new_charge) - 0.4 * jnp.tanh(new_over) - (0.2 * now) * new_film
            )
            misfit = seen - predicted
            gained += misfit * misfit
            fresh = (new_charge, new_over, new_heat, new_film)
            if step % STEPS_EPOCH == STEPS_EPOCH - 1:
                for c in range(STATES):
                    gather[q, pl.ds(c, ROWS, stride=STATES), :] = fresh[c]
            else:
                natural[q] = jnp.concatenate(fresh, axis=0).astype(jnp.bfloat16)
        total[...] += gained

    def finish(g):
        for q in members(g):
            lanes = pl.ds(pl.multiple_of(q * LANES, LANES), LANES)
            for j in range(ROWS):
                states[j, :, lanes] = gather[q, j * STATES : (j + 1) * STATES, :].astype(jnp.bfloat16)

    step = epoch * STEPS_EPOCH
    in_turn(assemble, functools.partial(spread_out, spread))
    in_turn(
        functools.partial(couple, spread),
        functools.partial(propagate, step),
        functools.partial(spread_out, spread_next),
    )
    in_turn(functools.partial(couple, spread_next), functools.partial(propagate, step + 1), finish)

    column = -0.5 * temper[0] * jnp.sum(total[...], axis=1, keepdims=True)
    slots = lax.broadcasted_iota(jnp.int32, (ROWS, LANES), 0)
    across_lanes = jnp.sum(jnp.where(slots == lane, column, 0.0), axis=0, keepdims=True)
    if epoch:
        logliks[0:1, :] = before[0:1, :]
    logliks[epoch : epoch + 1, :] = across_lanes


def weigh_kernel(own, other, log_weight, evidence):
    lane = lax.broadcasted_iota(jnp.int32, (EPOCHS, LANES), 1)
    real = lane < ROWS
    mine, theirs = own[...], other[...]
    peak = jnp.max(jnp.where(real, jnp.maximum(mine, theirs), -jnp.inf), axis=1, keepdims=True)
    shares = jnp.where(real, jnp.exp(mine - peak) + jnp.exp(theirs - peak), 0.0)
    lse = peak + jnp.log(jnp.sum(shares, axis=1, keepdims=True))
    log_weight[...] = (mine - lse)[:, :ROWS]
    per_cell = (lse - jnp.log(jnp.full(lse.shape, 2.0 * ROWS, jnp.float32))) / CELLS
    evidence[...] = jnp.sum(per_cell, axis=0, keepdims=True)


def on_device(
    particles, ancestors, migration, pattern, coupling, cell_rate, current, observed, noise_seeds
):
    shape = jax.ShapeDtypeStruct
    vector = shape((PAIRS, STATES * ROWS, LANES), jnp.float32)
    cost = pl.CostEstimate(flops=15000000, bytes_accessed=6000000, transcendentals=0)
    partner = from_partner(particles)
    sources = (noise_seeds, ancestors, migration, pattern.T, current, particles, coupling.transpose(1, 0, 2))
    halves = shape((NEIGH, BLOCKS // 2, BLOCK * BLOCK), jnp.bfloat16)
    sources = [in_hbm(x) for x in sources]
    noise, seeds, ancestors, migration, pattern, current, states, front, half, temper = pl.pallas_call(
        first_kernel,
        out_shape=(
            vector,
            *(pltpu.SMEM(x.shape, x.dtype) for x in sources[:5]),
            shape(particles.shape, particles.dtype),
            halves,
            pltpu.SMEM((1,), jnp.int32),
            pltpu.SMEM((1,), jnp.float32),
        ),
        in_specs=[HBM] * 7,
        out_specs=(VMEM, *[SMEM] * 5, VMEM, VMEM, SMEM, SMEM),
        scratch_shapes=[pltpu.SemaphoreType.DMA((7,))],
        compiler_params=params(2),
        cost_estimate=cost,
        name="first",
    )(*sources)

    logliks = ()
    rates = cell_rate.reshape(PAIRS, LANES)
    for epoch in range(EPOCHS):
        if epoch:
            partner = from_partner(states)
            noise = pl.pallas_call(
                noise_kernel,
                out_shape=(vector, vector),
                in_specs=[SMEM],
                out_specs=(VMEM, VMEM),
                compiler_params=params(2),
                cost_estimate=cost,
                name="noise",
            )(seeds)
        partner, noise = lax.optimization_barrier((partner, noise))
        leaving = pl.pallas_call(
            functools.partial(leaving_kernel, epoch),
            out_shape=shape((1, STATES, CELLS), jnp.bfloat16),
            in_specs=[SMEM, SMEM, SMEM, HBM, HBM],
            out_specs=HBM,
            scratch_shapes=[pltpu.SemaphoreType.DMA],
            compiler_params=params(1),
            name="leaving",
        )(ancestors, migration, half, states, partner)
        arriving = from_behind(leaving)
        if not epoch:
            leaving, seeds = lax.optimization_barrier((leaving, seeds))
            later, back = pl.pallas_call(
                second_kernel,
                out_shape=(vector, halves),
                in_specs=[SMEM, HBM],
                out_specs=(VMEM, VMEM),
                scratch_shapes=[pltpu.SemaphoreType.DMA],
                compiler_params=params(2),
                cost_estimate=cost,
                name="second",
            )(seeds, sources[6])
            noise = (noise, later)
            weights = pl.pallas_call(
                weights_kernel,
                out_shape=shape((BLOCKS // 4, NEIGH * BLOCK, 4 * BLOCK), jnp.bfloat16),
                in_specs=[VMEM, VMEM],
                out_specs=VMEM,
                scratch_shapes=[pltpu.VMEM((TURNS * NEIGH, HALF * 16, LANES), jnp.float32)],
                compiler_params=params(6),
                cost_estimate=pl.CostEstimate(flops=3000000, bytes_accessed=10000000, transcendentals=0),
                name="weights",
            )(front, back)
        states, logliks = pl.pallas_call(
            functools.partial(epoch_kernel, epoch),
            out_shape=(
                shape((ROWS, STATES, CELLS), jnp.bfloat16),
                shape((EPOCHS, LANES), jnp.float32),
            ),
            in_specs=[SMEM] * 6 + [VMEM] * (9 if epoch else 8),
            out_specs=(VMEM, VMEM),
            scratch_shapes=[
                pltpu.VMEM((PAIRS, STATES * ROWS, LANES), jnp.float32),
                pltpu.VMEM((PAIRS, STATES * ROWS, LANES), jnp.bfloat16),
                pltpu.VMEM((BLOCKS, STATES * ROWS, LANES), jnp.bfloat16),
                pltpu.VMEM((BLOCKS, STATES * ROWS, LANES), jnp.bfloat16),
                pltpu.VMEM((GROUP, STATES * ROWS, LANES), jnp.float32),
                pltpu.VMEM((LANES, 2 * LANES), jnp.bfloat16),
                pltpu.VMEM((ROWS, LANES), jnp.float32),
            ],
            compiler_params=params(12),
            name="epoch",
        )(
            ancestors,
            migration,
            half,
            pattern,
            current,
            temper,
            states,
            partner,
            arriving,
            weights,
            *noise,
            rates,
            observed,
            *([logliks] if epoch else []),
        )
    log_weight, evidence = pl.pallas_call(
        weigh_kernel,
        out_shape=(shape((EPOCHS, ROWS), jnp.float32), shape((1, 1), jnp.float32)),
        in_specs=[VMEM, VMEM],
        out_specs=(VMEM, VMEM),
        compiler_params=params(1),
        name="weigh",
    )(logliks, from_partner(logliks))
    return (states, evidence.reshape(1), log_weight)


def solution(mesh):
    return jax.shard_map(
        on_device,
        mesh=mesh,
        in_specs=(
            P(("group", "island"), None, None),
            P(None, ("group", "island"), None),
            P(None, ("group", "island"), None),
            P("group", None),
            P("group", None, None),
            P("group"),
            P("group"),
            P("group", None),
            P(("group", "island"), None),
        ),
        out_specs=(
            P(("group", "island"), None, None),
            P(("group", "island")),
            P(None, ("group", "island")),
        ),
        check_vma=False,
    )
```

```python
import functools

import jax
import jax.numpy as jnp
from jax import lax
from jax.experimental import pallas as pl
from jax.experimental.pallas import tpu as pltpu
from jax.sharding import PartitionSpec as P

CELLS = 8192
STATES = 4
BLOCK = 64
NEIGH = 5
EPOCHS = 2
STEPS_EPOCH = 2
STEPS = EPOCHS * STEPS_EPOCH
BLOCKS = 128
ROWS = 8
LANES = 128
TURNS = 2
GROUP = 16
PAIRS = CELLS // LANES
HALF = BLOCK // 2
NOISE_SCALE = 0.3 * 2.449489742783178 / 16777216.0

VMEM = pl.BlockSpec(memory_space=pltpu.VMEM)
SMEM = pl.BlockSpec(memory_space=pltpu.SMEM)
HBM = pl.BlockSpec(memory_space=pl.ANY)


def in_hbm(array):
    return pltpu.with_memory_space_constraint(array, pltpu.HBM)


def params(mib):
    return pltpu.CompilerParams(vmem_limit_bytes=mib << 20)


def from_partner(value):
    pairs = [(source, source ^ 1) for source in range(lax.axis_size("island"))]
    return lax.ppermute(value, "island", pairs)


def from_behind(block):
    count = lax.axis_size("island")
    route = [((i - 2) % count, i) for i in range(count)]
    return lax.ppermute(block, "island", route)


def shifted(hashed):
    return hashed ^ lax.shift_right_logical(hashed, jnp.full(hashed.shape, 16, jnp.int32))


def scramble(hashed):
    hashed = shifted(hashed) * 73244475
    hashed = shifted(hashed) * 73244475
    return shifted(hashed) & 16777215


def draw(seed, out):
    row = lax.broadcasted_iota(jnp.int32, (STATES * ROWS, LANES), 0)
    lane = lax.broadcasted_iota(jnp.int32, (STATES * ROWS, LANES), 1)
    start = 2 * (((row % ROWS) * STATES + row // ROWS) * CELLS + lane) + seed * 40503

    def one(q, carry):
        anchor = start + q * (2 * LANES)
        apart = scramble(anchor) - scramble(anchor + 1)
        rows = STATES * ROWS
        out[pl.ds(pl.multiple_of(q * rows, rows), rows), :] = apart.astype(jnp.float32) * NOISE_SCALE
        return carry

    lax.fori_loop(0, PAIRS, one, 0, unroll=4)


def first_kernel(*refs):
    sources, out, targets, (half, temper, sems) = refs[:7], refs[7], refs[8:15], refs[15:]
    sources = (*sources[:6], sources[6].at[:, : BLOCKS // 2])
    copies = [
        pltpu.make_async_copy(source, target, sems.at[i])
        for i, (source, target) in enumerate(zip(sources, targets))
    ]
    for copy in copies:
        copy.start()
    position = lax.axis_index("island")
    half[0] = position & 1
    temper[0] = 0.25 * lax.shift_left(jnp.int32(1), (position >> 1) & 3).astype(jnp.float32)
    for copy in copies[:5]:
        copy.wait()
    draw(targets[0][0, 0], out)
    for copy in copies[5:]:
        copy.wait()


def second_kernel(seeds, coupling, out, target, sem):
    copy = pltpu.make_async_copy(coupling.at[:, BLOCKS // 2 :], target, sem)
    copy.start()
    draw(seeds[0, 1], out)
    copy.wait()


def noise_kernel(seeds, *outs):
    for step, out in enumerate(outs):
        draw(seeds[0, STEPS_EPOCH + step], out)


def weights_kernel(front, back, out, wide):
    group = 16
    lane = lax.broadcasted_iota(jnp.int32, (1, LANES), 1)

    def move(coupling, g, local_g, k, held):
        for r in range(HALF):
            wide[held, r * group : (r + 1) * group, :] = coupling[
                k, pl.ds(pl.multiple_of(local_g * group, group), group), r * LANES : (r + 1) * LANES
            ].astype(jnp.float32)
        for b in range(0, group, 2):
            left, right = (wide[held, pl.ds(b + d, HALF, stride=group), :] for d in range(2))
            across = pltpu.roll(jnp.where(lane < BLOCK, right, left), BLOCK, 1)
            even, odd = jnp.where(lane < BLOCK, left, across), jnp.where(lane < BLOCK, across, right)
            out[
                g * (group // 4) + b // 4,
                k * BLOCK : (k + 1) * BLOCK,
                (b // 2 % 2) * LANES : (b // 2 % 2 + 1) * LANES,
            ] = jnp.concatenate([even, odd], axis=0).astype(jnp.bfloat16)

    groups = BLOCKS // 2 // group
    for part, coupling in enumerate((front, back)):

        def one(at, carry, part=part, coupling=coupling):
            for d in range(TURNS):
                g = TURNS * at + d
                for k in range(NEIGH):
                    move(coupling, part * groups + g, g, k, d * NEIGH + k)
            return carry

        lax.fori_loop(0, groups // TURNS, one, 0)


def leaving_kernel(epoch, ancestors, migration, half, local, partner, out, sem):
    chosen = ancestors[epoch, 0, migration[epoch, 0, 0]]
    slot = chosen % ROWS
    is_local = chosen // ROWS == half[0]

    @pl.when(is_local)
    def _():
        copy = pltpu.make_async_copy(local.at[pl.ds(slot, 1)], out, sem)
        copy.start()
        copy.wait()

    @pl.when(jnp.logical_not(is_local))
    def _():
        copy = pltpu.make_async_copy(partner.at[pl.ds(slot, 1)], out, sem)
        copy.start()
        copy.wait()


def advance(mixed, drawn, rate, seen, now):
    charge, over, heat, film = mixed
    tanh_over = jnp.tanh(over)
    fade = jnp.exp(-0.5 * jnp.abs(charge))
    warm = 0.6 * jnp.tanh(heat)
    rise = jnp.exp(warm + 2.0 * tanh_over) - jnp.exp(warm - 2.0 * tanh_over)
    reaction = (0.5 * rate) * rise * fade / (1.0 + fade * fade)
    new_charge = charge - 0.25 * reaction + drawn[0]
    new_over = 0.7 * over + 0.5 * (now - reaction) + drawn[1]
    new_heat = 0.9 * heat + 0.2 * reaction * tanh_over + drawn[2]
    new_film = 0.95 * film + 0.02 * reaction * reaction + drawn[3]
    predicted = 0.5 + 0.5 * jnp.tanh(0.5 * new_charge) - 0.4 * jnp.tanh(new_over) - (0.2 * now) * new_film
    return (new_charge, new_over, new_heat, new_film), seen - predicted


def fill_unmix(unmix):
    source = lax.broadcasted_iota(jnp.int32, (LANES, 2 * LANES), 0)
    target = lax.broadcasted_iota(jnp.int32, (LANES, 2 * LANES), 1)
    wanted = (target >> 7) * BLOCK + (target & (HALF - 1)) * 2 + ((target >> 5) & 1)
    unmix[...] = jnp.where(source == wanted, 1.0, 0.0).astype(jnp.bfloat16)


def inputs(load, pattern, b, lane):
    pieces = [load(pattern[k, b]) for k in range(NEIGH)]
    return jnp.concatenate(
        [
            jnp.where(lane < BLOCK, pieces[0], pieces[1]),
            jnp.where(lane < BLOCK, pieces[2], pieces[3]),
            pieces[4][:, :BLOCK],
        ],
        axis=1,
    )


def members(g):
    return [g * GROUP + i for i in range(GROUP)]


def in_turn(*stages):
    count = PAIRS // GROUP
    depth = len(stages)

    def one(at, low, high):
        for s in reversed(range(low, high)):
            stages[s](at - s)

    def steady(at, carry):
        one(at, 0, depth)
        return carry

    for at in range(depth - 1):
        one(at, 0, at + 1)
    lax.fori_loop(depth - 1, count, steady, 0, unroll=2)
    for at in range(count, count + depth - 1):
        one(at, at - count + 1, depth)


def epoch_kernel(
    epoch,
    ancestors,
    migration,
    half,
    pattern,
    current,
    temper,
    local,
    partner,
    weights,
    noise_first,
    noise_second,
    cell_rate,
    observed,
    *rest,
):
    if epoch:
        before, *rest, seen_rows = rest[:3] + rest[4:] + rest[3:4]
    else:
        arriving, *rest = rest
    states, logliks, gather, natural, spread, spread_next, coupled, unmix, total = rest
    lane = lax.broadcasted_iota(jnp.int32, (1, LANES), 1)

    fill_unmix(unmix)
    picks = []
    for j in range(ROWS):
        chosen = ancestors[epoch, 0, j]
        picks.append((chosen % ROWS, chosen // ROWS == half[0], migration[epoch, 0, 0] == j))

    rows = STATES * ROWS
    total[...] = jnp.zeros_like(total)

    def assemble(g):
        for q in members(g):
            lanes = pl.ds(pl.multiple_of(q * LANES, LANES), LANES)
            for j, (slot, is_local, is_new) in enumerate(picks):
                kept = jnp.where(
                    is_local,
                    local[slot, :, lanes].astype(jnp.float32),
                    partner[slot, :, lanes].astype(jnp.float32),
                )
                if not epoch:
                    kept = jnp.where(is_new, arriving[0, :, lanes].astype(jnp.float32), kept)
                gather[q, j * STATES : (j + 1) * STATES, :] = kept
            for c in range(0, STATES, 2):
                two = [gather[q, pl.ds(c + d, ROWS, stride=STATES), :] for d in range(2)]
                natural[q, c * ROWS : (c + 2) * ROWS, :] = jnp.concatenate(two, axis=0).astype(
                    jnp.bfloat16
                )

    def spread_out(result, g):
        cells = natural[pl.ds(g * GROUP, GROUP)].reshape(GROUP * rows, LANES)
        placed = jnp.dot(cells, unmix[...], preferred_element_type=jnp.float32).astype(jnp.bfloat16)
        for i, q in enumerate(members(g)):
            for side in range(2):
                result[2 * q + side] = placed[
                    i * rows : (i + 1) * rows, side * LANES : (side + 1) * LANES
                ]

    def couple(held, g):
        for i in range(0, GROUP, 2):
            quad = g * (GROUP // 2) + i // 2
            four = jnp.concatenate([inputs(lambda n: held[n], pattern, 4 * quad + d, lane) for d in range(4)], axis=0)
            product = jnp.dot(four, weights[quad], preferred_element_type=jnp.float32)
            for side in range(2):
                part = product[2 * side * rows : 2 * (side + 1) * rows, side * LANES : (side + 1) * LANES]
                coupled[i + side] = jnp.where(lane < BLOCK, part[:rows], part[rows:])

    def propagate(step, g):
        now = current[step]
        gained = jnp.zeros((ROWS, LANES), jnp.float32)
        for i, q in enumerate(members(g)):
            mixed = 0.6 * natural[q].astype(jnp.float32) + 0.8 * coupled[i]
            drawn = (noise_first, noise_second)[step % STEPS_EPOCH][
                pl.ds(pl.multiple_of(q * rows, rows), rows), :
            ]
            seen = observed[step : step + 1, pl.ds(pl.multiple_of(q * LANES, LANES), LANES)]
            if epoch:
                seen_rows[step % STEPS_EPOCH, pl.ds(q, 1), :] = seen
            parts = ([x[c * ROWS : (c + 1) * ROWS] for c in range(STATES)] for x in (mixed, drawn))
            fresh, misfit = advance(*parts, cell_rate[pl.ds(q, 1), :], seen, now)
            gained += misfit * misfit
            if step % STEPS_EPOCH == STEPS_EPOCH - 1:
                for c in range(STATES):
                    gather[q, pl.ds(c, ROWS, stride=STATES), :] = fresh[c]
            else:
                natural[q] = jnp.concatenate(fresh, axis=0).astype(jnp.bfloat16)
        total[...] += gained

    def finish(g):
        for q in members(g):
            lanes = pl.ds(pl.multiple_of(q * LANES, LANES), LANES)
            for j in range(ROWS):
                states[j, :, lanes] = gather[q, j * STATES : (j + 1) * STATES, :].astype(jnp.bfloat16)

    step = epoch * STEPS_EPOCH
    in_turn(assemble, functools.partial(spread_out, spread))
    in_turn(
        functools.partial(couple, spread),
        functools.partial(propagate, step),
        functools.partial(spread_out, spread_next),
    )
    in_turn(functools.partial(couple, spread_next), functools.partial(propagate, step + 1), finish)

    column = -0.5 * temper[0] * jnp.sum(total[...], axis=1, keepdims=True)
    slots = lax.broadcasted_iota(jnp.int32, (ROWS, LANES), 0)
    across_lanes = jnp.sum(jnp.where(slots == lane, column, 0.0), axis=0, keepdims=True)
    if epoch:
        logliks[0:1, :] = before[0:1, :]
    logliks[epoch : epoch + 1, :] = across_lanes


def migrant_kernel(
    migration,
    pattern,
    current,
    temper,
    arriving,
    weights,
    noise_first,
    noise_second,
    cell_rate,
    seen,
    before,
    _,
    logliks,
    states,
    rows,
    spread,
    unmix,
    result,
    sem,
):
    slot = migration[1, 0, 0]
    lane = lax.broadcasted_iota(jnp.int32, (1, LANES), 1)
    fill_unmix(unmix)
    for q in range(PAIRS):
        rows[ROWS * q : ROWS * q + STATES, :] = arriving[0, :, q * LANES : (q + 1) * LANES].astype(jnp.float32)
    channels = [pl.ds(c, PAIRS, stride=ROWS) for c in range(STATES)]
    held = [rows[channel, :] for channel in channels]
    total = jnp.zeros((PAIRS, LANES), jnp.float32)
    for inner in range(STEPS_EPOCH):
        placed = jnp.dot(
            jnp.concatenate(held, axis=0).astype(jnp.bfloat16), unmix[...], preferred_element_type=jnp.float32
        )
        for c in range(STATES):
            for side in range(2):
                spread[pl.ds(ROWS * side + c, PAIRS, stride=2 * ROWS), :] = placed[
                    c * PAIRS : (c + 1) * PAIRS, side * LANES : (side + 1) * LANES
                ]

        def block(n):
            return spread[pl.ds(pl.multiple_of(n * ROWS, ROWS), ROWS), :]

        for quad in range(BLOCKS // 4):
            four = jnp.concatenate([inputs(block, pattern, 4 * quad + d, lane) for d in range(4)], axis=0)
            product = jnp.dot(
                four.astype(jnp.bfloat16), weights[quad], preferred_element_type=jnp.float32
            )
            for side in range(2):
                part = product[2 * side * ROWS : 2 * (side + 1) * ROWS, side * LANES : (side + 1) * LANES]
                at = (2 * quad + side) * ROWS
                rows[at : at + ROWS, :] = jnp.where(lane < BLOCK, part[:ROWS], part[ROWS:])
        noise = (noise_first, noise_second)[inner]
        mixed = [0.6 * held[c] + 0.8 * rows[channels[c], :] for c in range(STATES)]
        drawn = [noise[pl.ds(c * ROWS + slot, PAIRS, stride=STATES * ROWS), :] for c in range(STATES)]
        fresh, misfit = advance(mixed, drawn, cell_rate[...], seen[inner], current[STEPS_EPOCH + inner])
        total += misfit * misfit
        held = [x.astype(jnp.bfloat16).astype(jnp.float32) for x in fresh]
    for c in range(STATES):
        rows[channels[c], :] = held[c]
    for q in range(PAIRS):
        result[0, :, q * LANES : (q + 1) * LANES] = rows[ROWS * q : ROWS * q + STATES, :].astype(jnp.bfloat16)
    copy = pltpu.make_async_copy(result, states.at[pl.ds(slot, 1)], sem)
    copy.start()
    gained = -0.5 * temper[0] * jnp.sum(jnp.sum(total, axis=0, keepdims=True), axis=1, keepdims=True)
    epochs = lax.broadcasted_iota(jnp.int32, (EPOCHS, LANES), 0)
    logliks[...] = jnp.where((epochs == 1) & (lane == slot), gained, before[...])
    copy.wait()


def weigh_kernel(own, other, log_weight, evidence):
    lane = lax.broadcasted_iota(jnp.int32, (EPOCHS, LANES), 1)
    real = lane < ROWS
    mine, theirs = own[...], other[...]
    peak = jnp.max(jnp.where(real, jnp.maximum(mine, theirs), -jnp.inf), axis=1, keepdims=True)
    shares = jnp.where(real, jnp.exp(mine - peak) + jnp.exp(theirs - peak), 0.0)
    lse = peak + jnp.log(jnp.sum(shares, axis=1, keepdims=True))
    log_weight[...] = (mine - lse)[:, :ROWS]
    per_cell = (lse - jnp.log(jnp.full(lse.shape, 2.0 * ROWS, jnp.float32))) / CELLS
    evidence[...] = jnp.sum(per_cell, axis=0, keepdims=True)


def on_device(
    particles, ancestors, migration, pattern, coupling, cell_rate, current, observed, noise_seeds
):
    shape = jax.ShapeDtypeStruct
    vector = shape((PAIRS * STATES * ROWS, LANES), jnp.float32)
    cost = pl.CostEstimate(flops=15000000, bytes_accessed=6000000, transcendentals=0)
    partner = from_partner(particles)
    sources = (noise_seeds, ancestors, migration, pattern.T, current, particles, coupling.transpose(1, 0, 2))
    halves = shape((NEIGH, BLOCKS // 2, BLOCK * BLOCK), jnp.bfloat16)
    sources = [in_hbm(x) for x in sources]
    noise, seeds, ancestors, migration, pattern, current, states, front, half, temper = pl.pallas_call(
        first_kernel,
        out_shape=(
            vector,
            *(pltpu.SMEM(x.shape, x.dtype) for x in sources[:5]),
            shape(particles.shape, particles.dtype),
            halves,
            pltpu.SMEM((1,), jnp.int32),
            pltpu.SMEM((1,), jnp.float32),
        ),
        in_specs=[HBM] * 7,
        out_specs=(VMEM, *[SMEM] * 5, VMEM, VMEM, SMEM, SMEM),
        scratch_shapes=[pltpu.SemaphoreType.DMA((7,))],
        compiler_params=params(2),
        cost_estimate=cost,
        name="first",
    )(*sources)

    logliks = ()
    rates = cell_rate.reshape(PAIRS, LANES)
    for epoch in range(EPOCHS):
        if epoch:
            partner = from_partner(states)
            noise = pl.pallas_call(
                noise_kernel,
                out_shape=(vector, vector),
                in_specs=[SMEM],
                out_specs=(VMEM, VMEM),
                compiler_params=params(2),
                cost_estimate=cost,
                name="noise",
            )(seeds)
        partner, noise = lax.optimization_barrier((partner, noise))
        leaving = pl.pallas_call(
            functools.partial(leaving_kernel, epoch),
            out_shape=shape((1, STATES, CELLS), jnp.bfloat16),
            in_specs=[SMEM, SMEM, SMEM, HBM, HBM],
            out_specs=HBM,
            scratch_shapes=[pltpu.SemaphoreType.DMA],
            compiler_params=params(1),
            name="leaving",
        )(ancestors, migration, half, states, partner)
        arriving = from_behind(leaving)
        if not epoch:
            leaving, seeds = lax.optimization_barrier((leaving, seeds))
            later, back = pl.pallas_call(
                second_kernel,
                out_shape=(vector, halves),
                in_specs=[SMEM, HBM],
                out_specs=(VMEM, VMEM),
                scratch_shapes=[pltpu.SemaphoreType.DMA],
                compiler_params=params(2),
                cost_estimate=cost,
                name="second",
            )(seeds, sources[6])
            noise = (noise, later)
            weights = pl.pallas_call(
                weights_kernel,
                out_shape=shape((BLOCKS // 4, NEIGH * BLOCK, 4 * BLOCK), jnp.bfloat16),
                in_specs=[VMEM, VMEM],
                out_specs=VMEM,
                scratch_shapes=[pltpu.VMEM((TURNS * NEIGH, HALF * 16, LANES), jnp.float32)],
                compiler_params=params(6),
                cost_estimate=pl.CostEstimate(flops=3000000, bytes_accessed=10000000, transcendentals=0),
                name="weights",
            )(front, back)
        states, logliks, *seen = pl.pallas_call(
            functools.partial(epoch_kernel, epoch),
            out_shape=(
                shape((ROWS, STATES, CELLS), jnp.bfloat16),
                shape((EPOCHS, LANES), jnp.float32),
                *([shape((STEPS_EPOCH, PAIRS, LANES), jnp.float32)] if epoch else []),
            ),
            in_specs=[SMEM] * 6 + [VMEM] * 8,
            out_specs=(VMEM, VMEM, *([VMEM] if epoch else [])),
            scratch_shapes=[
                pltpu.VMEM((PAIRS, STATES * ROWS, LANES), jnp.float32),
                pltpu.VMEM((PAIRS, STATES * ROWS, LANES), jnp.bfloat16),
                pltpu.VMEM((BLOCKS, STATES * ROWS, LANES), jnp.bfloat16),
                pltpu.VMEM((BLOCKS, STATES * ROWS, LANES), jnp.bfloat16),
                pltpu.VMEM((GROUP, STATES * ROWS, LANES), jnp.float32),
                pltpu.VMEM((LANES, 2 * LANES), jnp.bfloat16),
                pltpu.VMEM((ROWS, LANES), jnp.float32),
            ],
            compiler_params=params(12),
            cost_estimate=pl.CostEstimate(flops=400000000, bytes_accessed=20000000, transcendentals=1000000),
            name="epoch",
        )(
            ancestors,
            migration,
            half,
            pattern,
            current,
            temper,
            states,
            partner,
            weights,
            *noise,
            rates,
            observed,
            logliks if epoch else arriving,
        )
    logliks, states = pl.pallas_call(
        migrant_kernel,
        out_shape=(shape((EPOCHS, LANES), jnp.float32), shape((ROWS, STATES, CELLS), jnp.bfloat16)),
        in_specs=[SMEM] * 4 + [VMEM] * 7 + [HBM],
        out_specs=(VMEM, HBM),
        input_output_aliases={11: 1},
        scratch_shapes=[
            pltpu.VMEM((PAIRS * ROWS, LANES), jnp.float32),
            pltpu.VMEM((BLOCKS * ROWS, LANES), jnp.float32),
            pltpu.VMEM((LANES, 2 * LANES), jnp.bfloat16),
            pltpu.VMEM((1, STATES, CELLS), jnp.bfloat16),
            pltpu.SemaphoreType.DMA,
        ],
        compiler_params=params(6),
        name="migrant",
    )(
        migration,
        pattern,
        current,
        temper,
        arriving,
        weights,
        *noise,
        rates,
        *seen,
        logliks,
        states,
    )
    log_weight, evidence = pl.pallas_call(
        weigh_kernel,
        out_shape=(shape((EPOCHS, ROWS), jnp.float32), shape((1, 1), jnp.float32)),
        in_specs=[VMEM, VMEM],
        out_specs=(VMEM, VMEM),
        compiler_params=params(1),
        name="weigh",
    )(logliks, from_partner(logliks))
    return (states, evidence.reshape(1), log_weight)


def solution(mesh):
    return jax.shard_map(
        on_device,
        mesh=mesh,
        in_specs=(
            P(("group", "island"), None, None),
            P(None, ("group", "island"), None),
            P(None, ("group", "island"), None),
            P("group", None),
            P("group", None, None),
            P("group"),
            P("group"),
            P("group", None),
            P(("group", "island"), None),
        ),
        out_specs=(
            P(("group", "island"), None, None),
            P(("group", "island")),
            P(None, ("group", "island")),
        ),
        check_vma=False,
    )
```

```python
import functools

import jax
import jax.numpy as jnp
from jax import lax
from jax.experimental import pallas as pl
from jax.experimental.pallas import tpu as pltpu
from jax.sharding import PartitionSpec as P

CELLS = 8192
STATES = 4
BLOCK = 64
NEIGH = 5
EPOCHS = 2
STEPS_EPOCH = 2
STEPS = EPOCHS * STEPS_EPOCH
BLOCKS = 128
ROWS = 8
LANES = 128
TURNS = 2
GROUP = 16
PAIRS = CELLS // LANES
HALF = BLOCK // 2
NOISE_SCALE = 0.3 * 2.449489742783178 / 16777216.0

VMEM = pl.BlockSpec(memory_space=pltpu.VMEM)
SMEM = pl.BlockSpec(memory_space=pltpu.SMEM)
HBM = pl.BlockSpec(memory_space=pl.ANY)


def in_hbm(array):
    return pltpu.with_memory_space_constraint(array, pltpu.HBM)


def params(mib):
    return pltpu.CompilerParams(vmem_limit_bytes=mib << 20)


def from_partner(value):
    pairs = [(source, source ^ 1) for source in range(lax.axis_size("island"))]
    return lax.ppermute(value, "island", pairs)


def from_behind(block):
    count = lax.axis_size("island")
    route = [((i - 2) % count, i) for i in range(count)]
    return lax.ppermute(block, "island", route)


def shifted(hashed):
    return hashed ^ lax.shift_right_logical(hashed, jnp.full(hashed.shape, 16, jnp.int32))


def scramble(hashed):
    hashed = shifted(hashed) * 73244475
    hashed = shifted(hashed) * 73244475
    return shifted(hashed) & 16777215


def draw(seed, out):
    row = lax.broadcasted_iota(jnp.int32, (STATES * ROWS, LANES), 0)
    lane = lax.broadcasted_iota(jnp.int32, (STATES * ROWS, LANES), 1)
    start = 2 * (((row % ROWS) * STATES + row // ROWS) * CELLS + lane) + seed * 40503

    def one(q, carry):
        anchor = start + q * (2 * LANES)
        apart = scramble(anchor) - scramble(anchor + 1)
        rows = STATES * ROWS
        out[pl.ds(pl.multiple_of(q * rows, rows), rows), :] = apart.astype(jnp.float32) * NOISE_SCALE
        return carry

    lax.fori_loop(0, PAIRS, one, 0, unroll=4)


def first_kernel(*refs):
    sources, out, targets, (half, temper, sems) = refs[:7], refs[7], refs[8:15], refs[15:]
    sources = (*sources[:6], sources[6].at[:, : BLOCKS // 2])
    copies = [
        pltpu.make_async_copy(source, target, sems.at[i])
        for i, (source, target) in enumerate(zip(sources, targets))
    ]
    for copy in copies:
        copy.start()
    position = lax.axis_index("island")
    half[0] = position & 1
    temper[0] = 0.25 * lax.shift_left(jnp.int32(1), (position >> 1) & 3).astype(jnp.float32)
    for copy in copies[:5]:
        copy.wait()
    draw(targets[0][0, 0], out)
    for copy in copies[5:]:
        copy.wait()


def noise_kernel(seeds, *outs):
    for step, out in enumerate(outs):
        draw(seeds[0, STEPS_EPOCH + step], out)


def weights_kernel(seeds, front, coupling, out, noise, back, wide, sem):
    copy = pltpu.make_async_copy(coupling.at[:, BLOCKS // 2 :], back, sem)
    copy.start()
    group = 16
    lane = lax.broadcasted_iota(jnp.int32, (1, LANES), 1)

    def move(blocks, g, local_g, k, held):
        for r in range(HALF):
            wide[held, r * group : (r + 1) * group, :] = blocks[
                k, pl.ds(pl.multiple_of(local_g * group, group), group), r * LANES : (r + 1) * LANES
            ].astype(jnp.float32)
        for b in range(0, group, 2):
            left, right = (wide[held, pl.ds(b + d, HALF, stride=group), :] for d in range(2))
            across = pltpu.roll(jnp.where(lane < BLOCK, right, left), BLOCK, 1)
            even, odd = jnp.where(lane < BLOCK, left, across), jnp.where(lane < BLOCK, across, right)
            out[
                g * (group // 4) + b // 4,
                k * BLOCK : (k + 1) * BLOCK,
                (b // 2 % 2) * LANES : (b // 2 % 2 + 1) * LANES,
            ] = jnp.concatenate([even, odd], axis=0).astype(jnp.bfloat16)

    groups = BLOCKS // 2 // group
    for part, blocks in enumerate((front, back)):
        if part:
            draw(seeds[0, 1], noise)
            copy.wait()

        def one(at, carry, part=part, blocks=blocks):
            for d in range(TURNS):
                g = TURNS * at + d
                for k in range(NEIGH):
                    move(blocks, part * groups + g, g, k, d * NEIGH + k)
            return carry

        lax.fori_loop(0, groups // TURNS, one, 0)


def leaving_kernel(epoch, ancestors, migration, half, local, partner, out, sem):
    chosen = ancestors[epoch, 0, migration[epoch, 0, 0]]
    slot = chosen % ROWS
    is_local = chosen // ROWS == half[0]

    @pl.when(is_local)
    def _():
        copy = pltpu.make_async_copy(local.at[pl.ds(slot, 1)], out, sem)
        copy.start()
        copy.wait()

    @pl.when(jnp.logical_not(is_local))
    def _():
        copy = pltpu.make_async_copy(partner.at[pl.ds(slot, 1)], out, sem)
        copy.start()
        copy.wait()


def advance(mixed, drawn, rate, seen, now):
    charge, over, heat, film = mixed
    tanh_over = jnp.tanh(over)
    fade = jnp.exp(-0.5 * jnp.abs(charge))
    warm = 0.6 * jnp.tanh(heat)
    rise = jnp.exp(warm + 2.0 * tanh_over) - jnp.exp(warm - 2.0 * tanh_over)
    reaction = (0.5 * rate) * rise * fade / (1.0 + fade * fade)
    new_charge = charge - 0.25 * reaction + drawn[0]
    new_over = 0.7 * over + 0.5 * (now - reaction) + drawn[1]
    new_heat = 0.9 * heat + 0.2 * reaction * tanh_over + drawn[2]
    new_film = 0.95 * film + 0.02 * reaction * reaction + drawn[3]
    predicted = 0.5 + 0.5 * jnp.tanh(0.5 * new_charge) - 0.4 * jnp.tanh(new_over) - (0.2 * now) * new_film
    return (new_charge, new_over, new_heat, new_film), seen - predicted


def fill_unmix(unmix):
    source = lax.broadcasted_iota(jnp.int32, (LANES, 2 * LANES), 0)
    target = lax.broadcasted_iota(jnp.int32, (LANES, 2 * LANES), 1)
    wanted = (target >> 7) * BLOCK + (target & (HALF - 1)) * 2 + ((target >> 5) & 1)
    unmix[...] = jnp.where(source == wanted, 1.0, 0.0).astype(jnp.bfloat16)


def inputs(load, pattern, b, lane):
    pieces = [load(pattern[k, b]) for k in range(NEIGH)]
    return jnp.concatenate(
        [
            jnp.where(lane < BLOCK, pieces[0], pieces[1]),
            jnp.where(lane < BLOCK, pieces[2], pieces[3]),
            pieces[4][:, :BLOCK],
        ],
        axis=1,
    )


def members(g):
    return [g * GROUP + i for i in range(GROUP)]


def in_turn(*stages):
    count = PAIRS // GROUP
    depth = len(stages)

    def one(at, low, high):
        for s in reversed(range(low, high)):
            stages[s](at - s)

    def steady(at, carry):
        one(at, 0, depth)
        return carry

    for at in range(depth - 1):
        one(at, 0, at + 1)
    lax.fori_loop(depth - 1, count, steady, 0, unroll=2)
    for at in range(count, count + depth - 1):
        one(at, at - count + 1, depth)


def epoch_kernel(
    epoch,
    ancestors,
    migration,
    half,
    pattern,
    current,
    temper,
    local,
    partner,
    weights,
    noise_first,
    noise_second,
    cell_rate,
    observed,
    *rest,
):
    if epoch:
        before, *rest, seen_rows = rest[:3] + rest[4:] + rest[3:4]
    else:
        arriving, *rest = rest
    states, logliks, gather, natural, spread, spread_next, coupled, unmix, total = rest
    lane = lax.broadcasted_iota(jnp.int32, (1, LANES), 1)

    fill_unmix(unmix)
    picks = []
    for j in range(ROWS):
        chosen = ancestors[epoch, 0, j]
        picks.append((chosen % ROWS, chosen // ROWS == half[0], migration[epoch, 0, 0] == j))

    rows = STATES * ROWS
    total[...] = jnp.zeros_like(total)

    def assemble(g):
        for q in members(g):
            lanes = pl.ds(pl.multiple_of(q * LANES, LANES), LANES)
            for j, (slot, is_local, is_new) in enumerate(picks):
                kept = jnp.where(
                    is_local,
                    local[slot, :, lanes].astype(jnp.float32),
                    partner[slot, :, lanes].astype(jnp.float32),
                )
                if not epoch:
                    kept = jnp.where(is_new, arriving[0, :, lanes].astype(jnp.float32), kept)
                gather[q, j * STATES : (j + 1) * STATES, :] = kept
            for c in range(0, STATES, 2):
                two = [gather[q, pl.ds(c + d, ROWS, stride=STATES), :] for d in range(2)]
                natural[q, c * ROWS : (c + 2) * ROWS, :] = jnp.concatenate(two, axis=0).astype(
                    jnp.bfloat16
                )

    def spread_out(result, g):
        cells = natural[pl.ds(g * GROUP, GROUP)].reshape(GROUP * rows, LANES)
        placed = jnp.dot(cells, unmix[...], preferred_element_type=jnp.float32).astype(jnp.bfloat16)
        for i, q in enumerate(members(g)):
            for side in range(2):
                result[2 * q + side] = placed[
                    i * rows : (i + 1) * rows, side * LANES : (side + 1) * LANES
                ]

    def couple(held, g):
        for i in range(0, GROUP, 2):
            quad = g * (GROUP // 2) + i // 2
            four = jnp.concatenate([inputs(lambda n: held[n], pattern, 4 * quad + d, lane) for d in range(4)], axis=0)
            product = jnp.dot(four, weights[quad], preferred_element_type=jnp.float32)
            for side in range(2):
                part = product[2 * side * rows : 2 * (side + 1) * rows, side * LANES : (side + 1) * LANES]
                coupled[i + side] = jnp.where(lane < BLOCK, part[:rows], part[rows:])

    def propagate(step, g):
        now = current[step]
        gained = jnp.zeros((ROWS, LANES), jnp.float32)
        for i, q in enumerate(members(g)):
            mixed = 0.6 * natural[q].astype(jnp.float32) + 0.8 * coupled[i]
            drawn = (noise_first, noise_second)[step % STEPS_EPOCH][
                pl.ds(pl.multiple_of(q * rows, rows), rows), :
            ]
            seen = observed[step : step + 1, pl.ds(pl.multiple_of(q * LANES, LANES), LANES)]
            if epoch:
                seen_rows[step % STEPS_EPOCH, pl.ds(q, 1), :] = seen
            parts = ([x[c * ROWS : (c + 1) * ROWS] for c in range(STATES)] for x in (mixed, drawn))
            fresh, misfit = advance(*parts, cell_rate[pl.ds(q, 1), :], seen, now)
            gained += misfit * misfit
            if step % STEPS_EPOCH == STEPS_EPOCH - 1:
                for c in range(STATES):
                    gather[q, pl.ds(c, ROWS, stride=STATES), :] = fresh[c]
            else:
                natural[q] = jnp.concatenate(fresh, axis=0).astype(jnp.bfloat16)
        total[...] += gained

    def finish(g):
        for q in members(g):
            lanes = pl.ds(pl.multiple_of(q * LANES, LANES), LANES)
            for j in range(ROWS):
                states[j, :, lanes] = gather[q, j * STATES : (j + 1) * STATES, :].astype(jnp.bfloat16)

    step = epoch * STEPS_EPOCH
    in_turn(assemble, functools.partial(spread_out, spread))
    in_turn(
        functools.partial(couple, spread),
        functools.partial(propagate, step),
        functools.partial(spread_out, spread_next),
    )
    in_turn(functools.partial(couple, spread_next), functools.partial(propagate, step + 1), finish)

    column = -0.5 * temper[0] * jnp.sum(total[...], axis=1, keepdims=True)
    slots = lax.broadcasted_iota(jnp.int32, (ROWS, LANES), 0)
    across_lanes = jnp.sum(jnp.where(slots == lane, column, 0.0), axis=0, keepdims=True)
    if epoch:
        logliks[0:1, :] = before[0:1, :]
    logliks[epoch : epoch + 1, :] = across_lanes


def migrant_kernel(
    migration,
    pattern,
    current,
    temper,
    arriving,
    weights,
    noise_first,
    noise_second,
    cell_rate,
    seen,
    before,
    logliks,
    rows,
    spread,
    unmix,
):
    slot = migration[1, 0, 0]
    lane = lax.broadcasted_iota(jnp.int32, (1, LANES), 1)
    fill_unmix(unmix)
    for q in range(PAIRS):
        rows[ROWS * q : ROWS * q + STATES, :] = arriving[0, :, q * LANES : (q + 1) * LANES].astype(jnp.float32)
    channels = [pl.ds(c, PAIRS, stride=ROWS) for c in range(STATES)]
    held = [rows[channel, :] for channel in channels]
    total = jnp.zeros((PAIRS, LANES), jnp.float32)
    for inner in range(STEPS_EPOCH):
        placed = jnp.dot(
            jnp.concatenate(held, axis=0).astype(jnp.bfloat16), unmix[...], preferred_element_type=jnp.float32
        )
        for c in range(STATES):
            for side in range(2):
                spread[pl.ds(ROWS * side + c, PAIRS, stride=2 * ROWS), :] = placed[
                    c * PAIRS : (c + 1) * PAIRS, side * LANES : (side + 1) * LANES
                ]

        def block(n):
            return spread[pl.ds(pl.multiple_of(n * ROWS, ROWS), ROWS), :]

        for quad in range(BLOCKS // 4):
            four = jnp.concatenate([inputs(block, pattern, 4 * quad + d, lane) for d in range(4)], axis=0)
            product = jnp.dot(
                four.astype(jnp.bfloat16), weights[quad], preferred_element_type=jnp.float32
            )
            for side in range(2):
                part = product[2 * side * ROWS : 2 * (side + 1) * ROWS, side * LANES : (side + 1) * LANES]
                at = (2 * quad + side) * ROWS
                rows[at : at + ROWS, :] = jnp.where(lane < BLOCK, part[:ROWS], part[ROWS:])
        noise = (noise_first, noise_second)[inner]
        mixed = [0.6 * held[c] + 0.8 * rows[channels[c], :] for c in range(STATES)]
        drawn = [noise[pl.ds(c * ROWS + slot, PAIRS, stride=STATES * ROWS), :] for c in range(STATES)]
        fresh, misfit = advance(mixed, drawn, cell_rate[...], seen[inner], current[STEPS_EPOCH + inner])
        total += misfit * misfit
        held = [x.astype(jnp.bfloat16).astype(jnp.float32) for x in fresh]
    for c in range(STATES):
        rows[channels[c], :] = held[c]
    gained = -0.5 * temper[0] * jnp.sum(jnp.sum(total, axis=0, keepdims=True), axis=1, keepdims=True)
    epochs = lax.broadcasted_iota(jnp.int32, (EPOCHS, LANES), 0)
    logliks[...] = jnp.where((epochs == 1) & (lane == slot), gained, before[...])


def place_kernel(migration, rows, _, states, result, sem):
    for q in range(PAIRS):
        result[0, :, q * LANES : (q + 1) * LANES] = rows[ROWS * q : ROWS * q + STATES, :].astype(jnp.bfloat16)
    copy = pltpu.make_async_copy(result, states.at[pl.ds(migration[1, 0, 0], 1)], sem)
    copy.start()
    copy.wait()


def weigh_kernel(own, other, log_weight, evidence):
    lane = lax.broadcasted_iota(jnp.int32, (EPOCHS, LANES), 1)
    real = lane < ROWS
    mine, theirs = own[...], other[...]
    peak = jnp.max(jnp.where(real, jnp.maximum(mine, theirs), -jnp.inf), axis=1, keepdims=True)
    shares = jnp.where(real, jnp.exp(mine - peak) + jnp.exp(theirs - peak), 0.0)
    lse = peak + jnp.log(jnp.sum(shares, axis=1, keepdims=True))
    log_weight[...] = (mine - lse)[:, :ROWS]
    per_cell = (lse - jnp.log(jnp.full(lse.shape, 2.0 * ROWS, jnp.float32))) / CELLS
    evidence[...] = jnp.sum(per_cell, axis=0, keepdims=True)


def on_device(
    particles, ancestors, migration, pattern, coupling, cell_rate, current, observed, noise_seeds
):
    shape = jax.ShapeDtypeStruct
    vector = shape((PAIRS * STATES * ROWS, LANES), jnp.float32)
    cost = pl.CostEstimate(flops=15000000, bytes_accessed=6000000, transcendentals=0)
    partner = from_partner(particles)
    sources = (noise_seeds, ancestors, migration, pattern.T, current, particles, coupling.transpose(1, 0, 2))
    halves = shape((NEIGH, BLOCKS // 2, BLOCK * BLOCK), jnp.bfloat16)
    sources = [in_hbm(x) for x in sources]
    noise, seeds, ancestors, migration, pattern, current, states, front, half, temper = pl.pallas_call(
        first_kernel,
        out_shape=(
            vector,
            *(pltpu.SMEM(x.shape, x.dtype) for x in sources[:5]),
            shape(particles.shape, particles.dtype),
            halves,
            pltpu.SMEM((1,), jnp.int32),
            pltpu.SMEM((1,), jnp.float32),
        ),
        in_specs=[HBM] * 7,
        out_specs=(VMEM, *[SMEM] * 5, VMEM, VMEM, SMEM, SMEM),
        scratch_shapes=[pltpu.SemaphoreType.DMA((7,))],
        compiler_params=params(2),
        cost_estimate=cost,
        name="first",
    )(*sources)

    logliks = ()
    rates = cell_rate.reshape(PAIRS, LANES)
    for epoch in range(EPOCHS):
        if epoch:
            partner = from_partner(states)
            noise = pl.pallas_call(
                noise_kernel,
                out_shape=(vector, vector),
                in_specs=[SMEM],
                out_specs=(VMEM, VMEM),
                compiler_params=params(2),
                cost_estimate=cost,
                name="noise",
            )(seeds)
        partner, noise = lax.optimization_barrier((partner, noise))
        leaving = pl.pallas_call(
            functools.partial(leaving_kernel, epoch),
            out_shape=shape((1, STATES, CELLS), jnp.bfloat16),
            in_specs=[SMEM, SMEM, SMEM, HBM, HBM],
            out_specs=HBM,
            scratch_shapes=[pltpu.SemaphoreType.DMA],
            compiler_params=params(1),
            name="leaving",
        )(ancestors, migration, half, states, partner)
        arriving = from_behind(leaving)
        if not epoch:
            leaving, seeds = lax.optimization_barrier((leaving, seeds))
            weights, later = pl.pallas_call(
                weights_kernel,
                out_shape=(shape((BLOCKS // 4, NEIGH * BLOCK, 4 * BLOCK), jnp.bfloat16), vector),
                in_specs=[SMEM, VMEM, HBM],
                out_specs=(VMEM, VMEM),
                scratch_shapes=[
                    pltpu.VMEM(halves.shape, halves.dtype),
                    pltpu.VMEM((TURNS * NEIGH, HALF * 16, LANES), jnp.float32),
                    pltpu.SemaphoreType.DMA,
                ],
                compiler_params=params(8),
                cost_estimate=pl.CostEstimate(flops=18000000, bytes_accessed=16000000, transcendentals=0),
                name="weights",
            )(seeds, front, sources[6])
            noise = (noise, later)
        states, logliks, *seen = pl.pallas_call(
            functools.partial(epoch_kernel, epoch),
            out_shape=(
                shape((ROWS, STATES, CELLS), jnp.bfloat16),
                shape((EPOCHS, LANES), jnp.float32),
                *([shape((STEPS_EPOCH, PAIRS, LANES), jnp.float32)] if epoch else []),
            ),
            in_specs=[SMEM] * 6 + [VMEM] * 8,
            out_specs=(VMEM, VMEM, *([VMEM] if epoch else [])),
            scratch_shapes=[
                pltpu.VMEM((PAIRS, STATES * ROWS, LANES), jnp.float32),
                pltpu.VMEM((PAIRS, STATES * ROWS, LANES), jnp.bfloat16),
                pltpu.VMEM((BLOCKS, STATES * ROWS, LANES), jnp.bfloat16),
                pltpu.VMEM((BLOCKS, STATES * ROWS, LANES), jnp.bfloat16),
                pltpu.VMEM((GROUP, STATES * ROWS, LANES), jnp.float32),
                pltpu.VMEM((LANES, 2 * LANES), jnp.bfloat16),
                pltpu.VMEM((ROWS, LANES), jnp.float32),
            ],
            compiler_params=params(12),
            cost_estimate=pl.CostEstimate(flops=400000000, bytes_accessed=20000000, transcendentals=1000000),
            name="epoch",
        )(
            ancestors,
            migration,
            half,
            pattern,
            current,
            temper,
            states,
            partner,
            weights,
            *noise,
            rates,
            observed,
            logliks if epoch else arriving,
        )
    logliks, rows = pl.pallas_call(
        migrant_kernel,
        out_shape=(shape((EPOCHS, LANES), jnp.float32), shape((PAIRS * ROWS, LANES), jnp.float32)),
        in_specs=[SMEM] * 4 + [VMEM] * 7,
        out_specs=(VMEM, VMEM),
        scratch_shapes=[
            pltpu.VMEM((BLOCKS * ROWS, LANES), jnp.float32),
            pltpu.VMEM((LANES, 2 * LANES), jnp.bfloat16),
        ],
        compiler_params=params(4),
        name="migrant",
    )(migration, pattern, current, temper, arriving, weights, *noise, rates, *seen, logliks)
    other = from_partner(logliks)
    states = pl.pallas_call(
        place_kernel,
        out_shape=shape((ROWS, STATES, CELLS), jnp.bfloat16),
        in_specs=[SMEM, VMEM, HBM],
        out_specs=HBM,
        input_output_aliases={2: 0},
        scratch_shapes=[pltpu.VMEM((1, STATES, CELLS), jnp.bfloat16), pltpu.SemaphoreType.DMA],
        compiler_params=params(1),
        cost_estimate=pl.CostEstimate(flops=1000000, bytes_accessed=2000000, transcendentals=0),
        name="place",
    )(migration, rows, states)
    log_weight, evidence = pl.pallas_call(
        weigh_kernel,
        out_shape=(shape((EPOCHS, ROWS), jnp.float32), shape((1, 1), jnp.float32)),
        in_specs=[VMEM, VMEM],
        out_specs=(VMEM, VMEM),
        compiler_params=params(1),
        name="weigh",
    )(logliks, other)
    return (states, evidence.reshape(1), log_weight)


def solution(mesh):
    return jax.shard_map(
        on_device,
        mesh=mesh,
        in_specs=(
            P(("group", "island"), None, None),
            P(None, ("group", "island"), None),
            P(None, ("group", "island"), None),
            P("group", None),
            P("group", None, None),
            P("group"),
            P("group"),
            P("group", None),
            P(("group", "island"), None),
        ),
        out_specs=(
            P(("group", "island"), None, None),
            P(("group", "island")),
            P(None, ("group", "island")),
        ),
        check_vma=False,
    )
```

```python
import functools

import jax
import jax.numpy as jnp
from jax import lax
from jax.experimental import pallas as pl
from jax.experimental.pallas import tpu as pltpu
from jax.sharding import PartitionSpec as P

CELLS = 8192
STATES = 4
BLOCK = 64
NEIGH = 5
EPOCHS = 2
STEPS_EPOCH = 2
STEPS = EPOCHS * STEPS_EPOCH
BLOCKS = 128
ROWS = 8
LANES = 128
TURNS = 2
LAG = 1
GROUP = 8
PAIRS = CELLS // LANES
HALF = BLOCK // 2
NOISE_SCALE = 0.3 * 2.449489742783178 / 16777216.0

VMEM = pl.BlockSpec(memory_space=pltpu.VMEM)
SMEM = pl.BlockSpec(memory_space=pltpu.SMEM)
HBM = pl.BlockSpec(memory_space=pl.ANY)


def in_hbm(array):
    return pltpu.with_memory_space_constraint(array, pltpu.HBM)


def params(mib):
    return pltpu.CompilerParams(vmem_limit_bytes=mib << 20)


def from_partner(value):
    pairs = [(source, source ^ 1) for source in range(lax.axis_size("island"))]
    return lax.ppermute(value, "island", pairs)


def from_behind(block):
    count = lax.axis_size("island")
    route = [((i - 2) % count, i) for i in range(count)]
    return lax.ppermute(block, "island", route)


def shifted(hashed):
    return hashed ^ lax.shift_right_logical(hashed, jnp.full(hashed.shape, 16, jnp.int32))


def scramble(hashed):
    hashed = shifted(hashed) * 73244475
    hashed = shifted(hashed) * 73244475
    return shifted(hashed) & 16777215


def draw(seed, out):
    row = lax.broadcasted_iota(jnp.int32, (STATES * ROWS, LANES), 0)
    lane = lax.broadcasted_iota(jnp.int32, (STATES * ROWS, LANES), 1)
    start = 2 * (((row % ROWS) * STATES + row // ROWS) * CELLS + lane) + seed * 40503

    def one(q, carry):
        anchor = start + q * (2 * LANES)
        apart = scramble(anchor) - scramble(anchor + 1)
        rows = STATES * ROWS
        out[pl.ds(pl.multiple_of(q * rows, rows), rows), :] = apart.astype(jnp.float32) * NOISE_SCALE
        return carry

    lax.fori_loop(0, PAIRS, one, 0, unroll=4)


def first_kernel(*refs):
    sources, out, targets, (half, temper, sems) = refs[:7], refs[7], refs[8:15], refs[15:]
    sources = (*sources[:6], sources[6].at[:, : BLOCKS // 2])
    copies = [
        pltpu.make_async_copy(source, target, sems.at[i])
        for i, (source, target) in enumerate(zip(sources, targets))
    ]
    for copy in copies:
        copy.start()
    position = lax.axis_index("island")
    half[0] = position & 1
    temper[0] = 0.25 * lax.shift_left(jnp.int32(1), (position >> 1) & 3).astype(jnp.float32)
    for copy in copies[:5]:
        copy.wait()
    draw(targets[0][0, 0], out)
    for copy in copies[5:]:
        copy.wait()


def noise_kernel(seeds, *outs):
    for step, out in enumerate(outs):
        draw(seeds[0, STEPS_EPOCH + step], out)


def weights_kernel(seeds, front, coupling, out, noise, back, wide, sem):
    copy = pltpu.make_async_copy(coupling.at[:, BLOCKS // 2 :], back, sem)
    copy.start()
    group = 16
    lane = lax.broadcasted_iota(jnp.int32, (1, LANES), 1)

    def move(blocks, g, local_g, k, held):
        for r in range(HALF):
            wide[held, r * group : (r + 1) * group, :] = blocks[
                k, pl.ds(pl.multiple_of(local_g * group, group), group), r * LANES : (r + 1) * LANES
            ].astype(jnp.float32)
        for b in range(0, group, 2):
            left, right = (wide[held, pl.ds(b + d, HALF, stride=group), :] for d in range(2))
            across = pltpu.roll(jnp.where(lane < BLOCK, right, left), BLOCK, 1)
            even, odd = jnp.where(lane < BLOCK, left, across), jnp.where(lane < BLOCK, across, right)
            out[
                g * (group // 4) + b // 4,
                k * BLOCK : (k + 1) * BLOCK,
                (b // 2 % 2) * LANES : (b // 2 % 2 + 1) * LANES,
            ] = jnp.concatenate([even, odd], axis=0).astype(jnp.bfloat16)

    groups = BLOCKS // 2 // group
    for part, blocks in enumerate((front, back)):
        if part:
            draw(seeds[0, 1], noise)
            copy.wait()

        def one(at, carry, part=part, blocks=blocks):
            for d in range(TURNS):
                g = TURNS * at + d
                for k in range(NEIGH):
                    move(blocks, part * groups + g, g, k, d * NEIGH + k)
            return carry

        lax.fori_loop(0, groups // TURNS, one, 0)


def leaving_kernel(epoch, ancestors, migration, half, local, partner, out, sem):
    chosen = ancestors[epoch, 0, migration[epoch, 0, 0]]
    slot = chosen % ROWS
    is_local = chosen // ROWS == half[0]

    @pl.when(is_local)
    def _():
        copy = pltpu.make_async_copy(local.at[pl.ds(slot, 1)], out, sem)
        copy.start()
        copy.wait()

    @pl.when(jnp.logical_not(is_local))
    def _():
        copy = pltpu.make_async_copy(partner.at[pl.ds(slot, 1)], out, sem)
        copy.start()
        copy.wait()


def advance(mixed, drawn, rate, seen, now):
    charge, over, heat, film = mixed
    tanh_over = jnp.tanh(over)
    fade = jnp.exp(-0.5 * jnp.abs(charge))
    warm = 0.6 * jnp.tanh(heat)
    rise = jnp.exp(warm + 2.0 * tanh_over) - jnp.exp(warm - 2.0 * tanh_over)
    reaction = (0.5 * rate) * rise * fade / (1.0 + fade * fade)
    new_charge = charge - 0.25 * reaction + drawn[0]
    new_over = 0.7 * over + 0.5 * (now - reaction) + drawn[1]
    new_heat = 0.9 * heat + 0.2 * reaction * tanh_over + drawn[2]
    new_film = 0.95 * film + 0.02 * reaction * reaction + drawn[3]
    predicted = 0.5 + 0.5 * jnp.tanh(0.5 * new_charge) - 0.4 * jnp.tanh(new_over) - (0.2 * now) * new_film
    return (new_charge, new_over, new_heat, new_film), seen - predicted


def fill_unmix(unmix):
    source = lax.broadcasted_iota(jnp.int32, (LANES, 2 * LANES), 0)
    target = lax.broadcasted_iota(jnp.int32, (LANES, 2 * LANES), 1)
    wanted = (target >> 7) * BLOCK + (target & (HALF - 1)) * 2 + ((target >> 5) & 1)
    unmix[...] = jnp.where(source == wanted, 1.0, 0.0).astype(jnp.bfloat16)


def inputs(load, pattern, b, lane):
    pieces = [load(pattern[k, b]) for k in range(NEIGH)]
    return jnp.concatenate(
        [
            jnp.where(lane < BLOCK, pieces[0], pieces[1]),
            jnp.where(lane < BLOCK, pieces[2], pieces[3]),
            pieces[4][:, :BLOCK],
        ],
        axis=1,
    )


def members(g):
    return [g * GROUP + i for i in range(GROUP)]


def in_turn(*stages):
    count = PAIRS // GROUP
    for at in range(count + LAG * (len(stages) - 1)):
        for s in reversed(range(len(stages))):
            if 0 <= at - s * LAG < count:
                stages[s](at - s * LAG)


def epoch_kernel(
    epoch,
    ancestors,
    migration,
    half,
    pattern,
    current,
    temper,
    local,
    partner,
    weights,
    noise_first,
    noise_second,
    cell_rate,
    observed,
    *rest,
):
    if epoch:
        before, *rest, seen_rows = rest[:3] + rest[4:] + rest[3:4]
    else:
        arriving, *rest = rest
    states, logliks, gather, natural, spread, spread_next, coupled, unmix, total = rest
    lane = lax.broadcasted_iota(jnp.int32, (1, LANES), 1)

    fill_unmix(unmix)
    picks = []
    for j in range(ROWS):
        chosen = ancestors[epoch, 0, j]
        picks.append((chosen % ROWS, chosen // ROWS == half[0], migration[epoch, 0, 0] == j))

    rows = STATES * ROWS
    total[...] = jnp.zeros_like(total)

    def assemble(g):
        for q in members(g):
            lanes = pl.ds(pl.multiple_of(q * LANES, LANES), LANES)
            for j, (slot, is_local, is_new) in enumerate(picks):
                kept = jnp.where(
                    is_local,
                    local[slot, :, lanes].astype(jnp.float32),
                    partner[slot, :, lanes].astype(jnp.float32),
                )
                if not epoch:
                    kept = jnp.where(is_new, arriving[0, :, lanes].astype(jnp.float32), kept)
                gather[q, j * STATES : (j + 1) * STATES, :] = kept
            for c in range(0, STATES, 2):
                two = [gather[q, pl.ds(c + d, ROWS, stride=STATES), :] for d in range(2)]
                natural[q, c * ROWS : (c + 2) * ROWS, :] = jnp.concatenate(two, axis=0).astype(
                    jnp.bfloat16
                )

    def spread_out(result, g):
        cells = natural[pl.ds(g * GROUP, GROUP)].reshape(GROUP * rows, LANES)
        placed = jnp.dot(cells, unmix[...], preferred_element_type=jnp.float32).astype(jnp.bfloat16)
        for i, q in enumerate(members(g)):
            for side in range(2):
                result[2 * q + side] = placed[
                    i * rows : (i + 1) * rows, side * LANES : (side + 1) * LANES
                ]

    def couple(held, g):
        for i in range(0, GROUP, 2):
            quad = g * (GROUP // 2) + i // 2
            four = jnp.concatenate([inputs(lambda n: held[n], pattern, 4 * quad + d, lane) for d in range(4)], axis=0)
            product = jnp.dot(four, weights[quad], preferred_element_type=jnp.float32)
            for side in range(2):
                part = product[2 * side * rows : 2 * (side + 1) * rows, side * LANES : (side + 1) * LANES]
                coupled[g * GROUP + i + side] = jnp.where(lane < BLOCK, part[:rows], part[rows:])

    def propagate(step, g):
        now = current[step]
        gained = jnp.zeros((ROWS, LANES), jnp.float32)
        for i, q in enumerate(members(g)):
            mixed = 0.6 * natural[q].astype(jnp.float32) + 0.8 * coupled[q]
            drawn = (noise_first, noise_second)[step % STEPS_EPOCH][
                pl.ds(pl.multiple_of(q * rows, rows), rows), :
            ]
            seen = observed[step : step + 1, pl.ds(pl.multiple_of(q * LANES, LANES), LANES)]
            if epoch:
                seen_rows[step % STEPS_EPOCH, pl.ds(q, 1), :] = seen
            parts = ([x[c * ROWS : (c + 1) * ROWS] for c in range(STATES)] for x in (mixed, drawn))
            fresh, misfit = advance(*parts, cell_rate[pl.ds(q, 1), :], seen, now)
            gained += misfit * misfit
            if step % STEPS_EPOCH == STEPS_EPOCH - 1:
                for c in range(STATES):
                    gather[q, pl.ds(c, ROWS, stride=STATES), :] = fresh[c]
            else:
                natural[q] = jnp.concatenate(fresh, axis=0).astype(jnp.bfloat16)
        total[...] += gained

    def finish(g):
        for q in members(g):
            lanes = pl.ds(pl.multiple_of(q * LANES, LANES), LANES)
            for j in range(ROWS):
                states[j, :, lanes] = gather[q, j * STATES : (j + 1) * STATES, :].astype(jnp.bfloat16)

    step = epoch * STEPS_EPOCH
    in_turn(assemble, functools.partial(spread_out, spread))
    in_turn(
        functools.partial(couple, spread),
        functools.partial(propagate, step),
        functools.partial(spread_out, spread_next),
    )
    in_turn(functools.partial(couple, spread_next), functools.partial(propagate, step + 1), finish)

    column = -0.5 * temper[0] * jnp.sum(total[...], axis=1, keepdims=True)
    slots = lax.broadcasted_iota(jnp.int32, (ROWS, LANES), 0)
    across_lanes = jnp.sum(jnp.where(slots == lane, column, 0.0), axis=0, keepdims=True)
    if epoch:
        logliks[0:1, :] = before[0:1, :]
    logliks[epoch : epoch + 1, :] = across_lanes


def migrant_kernel(
    migration,
    pattern,
    current,
    temper,
    arriving,
    weights,
    noise_first,
    noise_second,
    cell_rate,
    seen,
    before,
    logliks,
    rows,
    spread,
    unmix,
):
    slot = migration[1, 0, 0]
    lane = lax.broadcasted_iota(jnp.int32, (1, LANES), 1)
    fill_unmix(unmix)
    for q in range(PAIRS):
        rows[ROWS * q : ROWS * q + STATES, :] = arriving[0, :, q * LANES : (q + 1) * LANES].astype(jnp.float32)
    channels = [pl.ds(c, PAIRS, stride=ROWS) for c in range(STATES)]
    held = [rows[channel, :] for channel in channels]
    total = jnp.zeros((PAIRS, LANES), jnp.float32)
    for inner in range(STEPS_EPOCH):
        placed = jnp.dot(
            jnp.concatenate(held, axis=0).astype(jnp.bfloat16), unmix[...], preferred_element_type=jnp.float32
        )
        for c in range(STATES):
            for side in range(2):
                spread[pl.ds(ROWS * side + c, PAIRS, stride=2 * ROWS), :] = placed[
                    c * PAIRS : (c + 1) * PAIRS, side * LANES : (side + 1) * LANES
                ]

        def block(n):
            return spread[pl.ds(pl.multiple_of(n * ROWS, ROWS), ROWS), :]

        for quad in range(BLOCKS // 4):
            four = jnp.concatenate([inputs(block, pattern, 4 * quad + d, lane) for d in range(4)], axis=0)
            product = jnp.dot(
                four.astype(jnp.bfloat16), weights[quad], preferred_element_type=jnp.float32
            )
            for side in range(2):
                part = product[2 * side * ROWS : 2 * (side + 1) * ROWS, side * LANES : (side + 1) * LANES]
                at = (2 * quad + side) * ROWS
                rows[at : at + ROWS, :] = jnp.where(lane < BLOCK, part[:ROWS], part[ROWS:])
        noise = (noise_first, noise_second)[inner]
        mixed = [0.6 * held[c] + 0.8 * rows[channels[c], :] for c in range(STATES)]
        drawn = [noise[pl.ds(c * ROWS + slot, PAIRS, stride=STATES * ROWS), :] for c in range(STATES)]
        fresh, misfit = advance(mixed, drawn, cell_rate[...], seen[inner], current[STEPS_EPOCH + inner])
        total += misfit * misfit
        held = [x.astype(jnp.bfloat16).astype(jnp.float32) for x in fresh]
    for c in range(STATES):
        rows[channels[c], :] = held[c]
    gained = -0.5 * temper[0] * jnp.sum(jnp.sum(total, axis=0, keepdims=True), axis=1, keepdims=True)
    epochs = lax.broadcasted_iota(jnp.int32, (EPOCHS, LANES), 0)
    logliks[...] = jnp.where((epochs == 1) & (lane == slot), gained, before[...])


def place_kernel(migration, rows, _, states, result, sem):
    for q in range(PAIRS):
        result[0, :, q * LANES : (q + 1) * LANES] = rows[ROWS * q : ROWS * q + STATES, :].astype(jnp.bfloat16)
    copy = pltpu.make_async_copy(result, states.at[pl.ds(migration[1, 0, 0], 1)], sem)
    copy.start()
    copy.wait()


def weigh_kernel(own, other, log_weight, evidence):
    lane = lax.broadcasted_iota(jnp.int32, (EPOCHS, LANES), 1)
    real = lane < ROWS
    mine, theirs = own[...], other[...]
    peak = jnp.max(jnp.where(real, jnp.maximum(mine, theirs), -jnp.inf), axis=1, keepdims=True)
    shares = jnp.where(real, jnp.exp(mine - peak) + jnp.exp(theirs - peak), 0.0)
    lse = peak + jnp.log(jnp.sum(shares, axis=1, keepdims=True))
    log_weight[...] = (mine - lse)[:, :ROWS]
    per_cell = (lse - jnp.log(jnp.full(lse.shape, 2.0 * ROWS, jnp.float32))) / CELLS
    evidence[...] = jnp.sum(per_cell, axis=0, keepdims=True)


def on_device(
    particles, ancestors, migration, pattern, coupling, cell_rate, current, observed, noise_seeds
):
    shape = jax.ShapeDtypeStruct
    vector = shape((PAIRS * STATES * ROWS, LANES), jnp.float32)
    cost = pl.CostEstimate(flops=15000000, bytes_accessed=6000000, transcendentals=0)
    partner = from_partner(particles)
    sources = (noise_seeds, ancestors, migration, pattern.T, current, particles, coupling.transpose(1, 0, 2))
    halves = shape((NEIGH, BLOCKS // 2, BLOCK * BLOCK), jnp.bfloat16)
    sources = [in_hbm(x) for x in sources]
    noise, seeds, ancestors, migration, pattern, current, states, front, half, temper = pl.pallas_call(
        first_kernel,
        out_shape=(
            vector,
            *(pltpu.SMEM(x.shape, x.dtype) for x in sources[:5]),
            shape(particles.shape, particles.dtype),
            halves,
            pltpu.SMEM((1,), jnp.int32),
            pltpu.SMEM((1,), jnp.float32),
        ),
        in_specs=[HBM] * 7,
        out_specs=(VMEM, *[SMEM] * 5, VMEM, VMEM, SMEM, SMEM),
        scratch_shapes=[pltpu.SemaphoreType.DMA((7,))],
        compiler_params=params(2),
        cost_estimate=cost,
        name="first",
    )(*sources)

    logliks = ()
    rates = cell_rate.reshape(PAIRS, LANES)
    for epoch in range(EPOCHS):
        if epoch:
            partner = from_partner(states)
            noise = pl.pallas_call(
                noise_kernel,
                out_shape=(vector, vector),
                in_specs=[SMEM],
                out_specs=(VMEM, VMEM),
                compiler_params=params(2),
                cost_estimate=cost,
                name="noise",
            )(seeds)
        partner, noise = lax.optimization_barrier((partner, noise))
        leaving = pl.pallas_call(
            functools.partial(leaving_kernel, epoch),
            out_shape=shape((1, STATES, CELLS), jnp.bfloat16),
            in_specs=[SMEM, SMEM, SMEM, HBM, HBM],
            out_specs=HBM,
            scratch_shapes=[pltpu.SemaphoreType.DMA],
            compiler_params=params(1),
            name="leaving",
        )(ancestors, migration, half, states, partner)
        arriving = from_behind(leaving)
        if not epoch:
            leaving, seeds = lax.optimization_barrier((leaving, seeds))
            weights, later = pl.pallas_call(
                weights_kernel,
                out_shape=(shape((BLOCKS // 4, NEIGH * BLOCK, 4 * BLOCK), jnp.bfloat16), vector),
                in_specs=[SMEM, VMEM, HBM],
                out_specs=(VMEM, VMEM),
                scratch_shapes=[
                    pltpu.VMEM(halves.shape, halves.dtype),
                    pltpu.VMEM((TURNS * NEIGH, HALF * 16, LANES), jnp.float32),
                    pltpu.SemaphoreType.DMA,
                ],
                compiler_params=params(8),
                cost_estimate=pl.CostEstimate(flops=18000000, bytes_accessed=16000000, transcendentals=0),
                name="weights",
            )(seeds, front, sources[6])
            noise = (noise, later)
        states, logliks, *seen = pl.pallas_call(
            functools.partial(epoch_kernel, epoch),
            out_shape=(
                shape((ROWS, STATES, CELLS), jnp.bfloat16),
                shape((EPOCHS, LANES), jnp.float32),
                *([shape((STEPS_EPOCH, PAIRS, LANES), jnp.float32)] if epoch else []),
            ),
            in_specs=[SMEM] * 6 + [VMEM] * 8,
            out_specs=(VMEM, VMEM, *([VMEM] if epoch else [])),
            scratch_shapes=[
                pltpu.VMEM((PAIRS, STATES * ROWS, LANES), jnp.float32),
                pltpu.VMEM((PAIRS, STATES * ROWS, LANES), jnp.bfloat16),
                pltpu.VMEM((BLOCKS, STATES * ROWS, LANES), jnp.bfloat16),
                pltpu.VMEM((BLOCKS, STATES * ROWS, LANES), jnp.bfloat16),
                pltpu.VMEM((PAIRS, STATES * ROWS, LANES), jnp.float32),
                pltpu.VMEM((LANES, 2 * LANES), jnp.bfloat16),
                pltpu.VMEM((ROWS, LANES), jnp.float32),
            ],
            compiler_params=params(12),
            cost_estimate=pl.CostEstimate(flops=400000000, bytes_accessed=20000000, transcendentals=1000000),
            name="epoch",
        )(
            ancestors,
            migration,
            half,
            pattern,
            current,
            temper,
            states,
            partner,
            weights,
            *noise,
            rates,
            observed,
            logliks if epoch else arriving,
        )
    logliks, rows = pl.pallas_call(
        migrant_kernel,
        out_shape=(shape((EPOCHS, LANES), jnp.float32), shape((PAIRS * ROWS, LANES), jnp.float32)),
        in_specs=[SMEM] * 4 + [VMEM] * 7,
        out_specs=(VMEM, VMEM),
        scratch_shapes=[
            pltpu.VMEM((BLOCKS * ROWS, LANES), jnp.float32),
            pltpu.VMEM((LANES, 2 * LANES), jnp.bfloat16),
        ],
        compiler_params=params(4),
        name="migrant",
    )(migration, pattern, current, temper, arriving, weights, *noise, rates, *seen, logliks)
    other = from_partner(logliks)
    states = pl.pallas_call(
        place_kernel,
        out_shape=shape((ROWS, STATES, CELLS), jnp.bfloat16),
        in_specs=[SMEM, VMEM, HBM],
        out_specs=HBM,
        input_output_aliases={2: 0},
        scratch_shapes=[pltpu.VMEM((1, STATES, CELLS), jnp.bfloat16), pltpu.SemaphoreType.DMA],
        compiler_params=params(1),
        cost_estimate=pl.CostEstimate(flops=1000000, bytes_accessed=2000000, transcendentals=0),
        name="place",
    )(migration, rows, states)
    log_weight, evidence = pl.pallas_call(
        weigh_kernel,
        out_shape=(shape((EPOCHS, ROWS), jnp.float32), shape((1, 1), jnp.float32)),
        in_specs=[VMEM, VMEM],
        out_specs=(VMEM, VMEM),
        compiler_params=params(1),
        name="weigh",
    )(logliks, other)
    return (states, evidence.reshape(1), log_weight)


def solution(mesh):
    return jax.shard_map(
        on_device,
        mesh=mesh,
        in_specs=(
            P(("group", "island"), None, None),
            P(None, ("group", "island"), None),
            P(None, ("group", "island"), None),
            P("group", None),
            P("group", None, None),
            P("group"),
            P("group"),
            P("group", None),
            P(("group", "island"), None),
        ),
        out_specs=(
            P(("group", "island"), None, None),
            P(("group", "island")),
            P(None, ("group", "island")),
        ),
        check_vma=False,
    )
```
